128 devices in a mesh: row: 4 (over x), col: 32 (over y, z, core).
Axes of the slice: x: 4, y: 4, z: 4, core: 2. Of those that a mesh axis runs over, the one named last changes fastest.
Arguments:
- resident_cell: int32 [8388608], P(('row', 'col')), may hold values from 0 to 16383
- resident_corner: int32 [8388608], P(('row', 'col')), may hold values from 0 to 7
- resident_frac: float32 [3, 8388608], P(None, ('row', 'col')), may hold values from 0 to 0.5
- resident_charge: float32 [8388608], P(('row', 'col')), may hold values from 0.5 to 2
- resident_momentum: float32 [3, 8388608], P(None, ('row', 'col')), may hold values from -6 to 6
- migrant_dest: int32 [262144, 1], P(('row', 'col')), may hold values from 0 to 31; in each aligned block of 2048 rows (0 to 2047, 2048 to 4095, ...) at most 128 rows name the same one
- migrant_cell: int32 [262144], P(('row', 'col')), may hold values from 0 to 16383
- migrant_corner: int32 [262144], P(('row', 'col')), may hold values from 0 to 7
- migrant_frac: float32 [3, 262144], P(None, ('row', 'col')), may hold values from 0 to 0.5
- migrant_charge: float32 [262144], P(('row', 'col')), may hold values from 0.5 to 2
- migrant_momentum: float32 [3, 262144], P(None, ('row', 'col')), may hold values from -6 to 6
- green: bfloat16 [3, 2, 256, 256, 256], P(None, None, ('row', 'col')), may hold values from -6 to 6
Outputs:
- resident_kicked: float32 [3, 8388608], P(None, ('row', 'col'))
- migrant_kicked: float32 [3, 524288], P(None, ('row', 'col'))
The draws below stay inside these ranges and needn't reach their ends.
Inputs may be any that keep to these rules, and one draw needn't show every extreme that they name: `migrant_dest`: among the rows of one device each destination is named by at most 128 rows, and some device names one destination in exactly 128 of its rows.
All inputs are finite; a program needn't handle non-finite values.
Results may differ from the reference program's by a relative error of at most 0.0003.
Values sent between devices are 32-bit elements; how exact they have to be, the bound alone decides.
A program may use at most 64 MiB of HBM per device.

```python
import math
import jax
import jax.numpy as jnp
import numpy as np

NG = 128
MG = 256
CY = 32
CZ = 4
RES_DEV = 65536
MIG_DEV = 2048
CAP = 128
RESIDENTS = 8388608
MIGRANTS = 262144
SLOTS = 524288
N_ROW = 4
N_COL = 32


def place_ends(drawn, rng, low, largest):
    place = [jax.random.randint(jax.random.fold_in(rng, axis), (), 0, length) for axis, length in enumerate(drawn.shape)]
    widest = drawn.shape.index(max(drawn.shape))
    neighbour = place[:widest] + [(place[widest] + 1) % drawn.shape[widest]] + place[widest + 1:]
    return drawn.at[tuple(place)].set(low).at[tuple(neighbour)].set(largest)


def block_scale(rng, shape, split, low, largest):
    level, own = 1.0, jax.random.fold_in(rng, 6)
    for dim, shards_of in split:
        draws = jnp.exp(jax.random.uniform(jax.random.fold_in(own, dim), (shards_of,), jnp.float32, low / len(split), largest / len(split)))
        level = level * jnp.repeat(draws, shape[dim] // shards_of).reshape([-1 if axis == dim else 1 for axis in range(len(shape))])
    return level


def routed_block(key, own, number, rows, number_of, top, bound, skew):
    ranking = jax.random.permutation(key, number_of)
    crowded, usual = load_shares(number_of, rows * top, bound, skew, True), load_shares(number_of, rows * top, bound, skew, False)
    places = jnp.arange(number_of)

    def named(lengths, offset_by):
        used = int((lengths > 0).sum())
        fixed = max(1, used // 4)
        shifted = fixed + (places - fixed + offset_by * (used - fixed)) % max(1, number_of - fixed)
        return jnp.zeros((number_of,), jnp.int32).at[ranking[jnp.where(places < fixed, places, shifted)]].set(jnp.asarray(lengths, jnp.int32))

    lengths = jnp.where(number % 4 == 0, named(crowded, number // 4), named(usual, number - number // 4 - 1))
    mixed = jax.random.permutation(jax.random.fold_in(own, 3), number_of)
    donor, taker = mixed[0:number_of // 2 * 2:2], mixed[1:number_of // 2 * 2:2]
    slack = jnp.minimum(lengths[donor] - 1, bound - lengths[taker]) // 2
    slack = jnp.where((donor == ranking[0]) | (taker == ranking[0]) | (lengths[taker] == 0), 0, jnp.maximum(slack, 0))
    shifted = jax.random.randint(jax.random.fold_in(own, 4), (number_of // 2,), 0, 1 << 20) % (slack + 1)
    lengths = lengths.at[donor].add(-shifted).at[taker].add(shifted)
    items = jnp.searchsorted(jnp.cumsum(lengths), jnp.arange(rows * top), side="right").astype(jnp.int32)
    listing = items.reshape(top, rows).T
    listing = listing[jax.random.permutation(jax.random.fold_in(own, 1), rows)]
    offset_by = jax.random.randint(jax.random.fold_in(own, 2), (rows, 1), 0, top)
    return jnp.take_along_axis(listing, (jnp.arange(top)[None, :] + offset_by) % top, axis=1)


def load_shares(number_of, total, limit, skew, full):
    portions = [(1 << 20) // math.isqrt(standing ** skew) + 1 for standing in range(1, number_of + 1)]
    largest = limit if full else min(limit, max(-(-total // number_of), total * portions[0] // sum(portions)))
    least = 1 if total - largest >= number_of - 1 else 0
    counts, rest = [largest] + [least] * (number_of - 1), total - largest - least * (number_of - 1)
    while rest > 0:
        candidates = [i for i in range(1, number_of) if counts[i] < largest] or [i for i in range(1, number_of) if counts[i] < limit]
        pool, left = sum([portions[i] for i in candidates]), rest
        for i in candidates:
            addition = min(limit - counts[i], max(1, left * portions[i] // pool), rest)
            counts[i] = counts[i] + addition
            rest = rest - addition
    return np.array(counts)


def scatter_about(own_key, shape, spread, reach, pieces=(), kind=jnp.bfloat16):
    array = jax.random.normal(own_key, shape, jnp.float32) * spread
    if len(pieces) > 0:
        array = block_scale(own_key, shape, pieces, -0.22, 0.18) * array
    return jnp.clip(array, min=-reach, max=reach).astype(kind)


def setup_inputs(seed: int = 0) -> dict:
    key_list = jax.random.split(jax.random.key(seed), 13)
    resident_cell = place_ends(jax.random.randint(key_list[0], (RESIDENTS,), 0, NG * NG * NG // (N_ROW * N_COL)), jax.random.fold_in(key_list[0], 1), 0, (NG * NG * NG // (N_ROW * N_COL)) - 1).astype(jnp.int32)
    resident_corner = place_ends(jax.random.randint(key_list[1], (RESIDENTS,), 0, 8), jax.random.fold_in(key_list[1], 1), 0, 7).astype(jnp.int32)
    resident_frac = jnp.clip(0.5 * jax.random.uniform(key_list[2], (3, RESIDENTS), jnp.float32) ** block_scale(key_list[2], (3, RESIDENTS), ((1, 128),), -0.2, 0.2), 0.0, 0.5)
    resident_charge = jnp.clip(jnp.exp(math.log(2.0) - 1.3862944 * jax.random.uniform(key_list[3], (RESIDENTS,), jnp.float32) ** block_scale(key_list[3], (RESIDENTS,), ((0, 128),), -0.2, 0.2)), 0.5, 2.0)
    resident_momentum = scatter_about(key_list[4], (3, RESIDENTS), 1.0, 6.0, ((1, 128),), jnp.float32)
    migrant_dest_keys = jax.random.split(jax.random.fold_in(key_list[5], 1), MIGRANTS // MIG_DEV)
    migrant_dest_turns = jax.random.permutation(jax.random.fold_in(key_list[5], 3), MIGRANTS // MIG_DEV)
    migrant_dest = jax.vmap(lambda own, number: routed_block(jax.random.fold_in(key_list[5], 2), own, number, MIG_DEV, N_COL, 1, CAP, 2))(migrant_dest_keys, migrant_dest_turns).reshape((MIGRANTS, 1))
    migrant_cell = place_ends(jax.random.randint(key_list[6], (MIGRANTS,), 0, NG * NG * NG // (N_ROW * N_COL)), jax.random.fold_in(key_list[6], 1), 0, (NG * NG * NG // (N_ROW * N_COL)) - 1).astype(jnp.int32)
    migrant_corner = place_ends(jax.random.randint(key_list[7], (MIGRANTS,), 0, 8), jax.random.fold_in(key_list[7], 1), 0, 7).astype(jnp.int32)
    migrant_frac = jnp.clip(0.5 * jax.random.uniform(key_list[8], (3, MIGRANTS), jnp.float32) ** block_scale(key_list[8], (3, MIGRANTS), ((1, 128),), -0.2, 0.2), 0.0, 0.5)
    migrant_charge = jnp.clip(jnp.exp(math.log(2.0) - 1.3862944 * jax.random.uniform(key_list[9], (MIGRANTS,), jnp.float32) ** block_scale(key_list[9], (MIGRANTS,), ((0, 128),), -0.2, 0.2)), 0.5, 2.0)
    migrant_momentum = scatter_about(key_list[10], (3, MIGRANTS), 1.0, 6.0, ((1, 128),), jnp.float32)
    green = scatter_about(key_list[11], (3, 2, MG, MG, MG), 1.0, 6.0, ((2, 128),))
    return {"resident_cell": resident_cell, "resident_corner": resident_corner, "resident_frac": resident_frac, "resident_charge": resident_charge, "resident_momentum": resident_momentum, "migrant_dest": migrant_dest, "migrant_cell": migrant_cell, "migrant_corner": migrant_corner, "migrant_frac": migrant_frac, "migrant_charge": migrant_charge, "migrant_momentum": migrant_momentum, "green": green}


def global_cells(cell_index, row_number, col_number):
    x_cell = cell_index % NG
    y_cell = row_number * CY + (cell_index // NG) % CY
    z_cell = col_number * CZ + cell_index // (NG * CY)
    return (x_cell, y_cell, z_cell)


def corner_list(coords, corner_code, frac_rows):
    per_dimension = []
    for dimension in range(3):
        side_sign = 2 * ((corner_code // (1, 2, 4)[dimension]) % 2) - 1
        per_dimension.append(((coords[dimension], 1.0 - frac_rows[dimension]), (coords[dimension] + side_sign, frac_rows[dimension])))
    listed = []
    for along_x in per_dimension[0]:
        for along_y in per_dimension[1]:
            for along_z in per_dimension[2]:
                flat_index = ((along_z[0] + 1) * (NG + 2) + along_y[0] + 1) * (NG + 2) + along_x[0] + 1
                listed.append((flat_index.astype(jnp.int32), along_x[1] * along_y[1] * along_z[1]))
    return listed


def corner_sum(listed, field_flat):
    running = jnp.zeros_like(listed[0][1])
    for flat_index, weight in listed:
        running = running + weight * field_flat[flat_index]
    return running


def reference(resident_cell, resident_corner, resident_frac, resident_charge, resident_momentum, migrant_dest, migrant_cell, migrant_corner, migrant_frac, migrant_charge, migrant_momentum, green):
    device_total = N_ROW * N_COL
    res_block = (jnp.arange(RESIDENTS, dtype=jnp.int32) // RES_DEV).astype(jnp.int32)
    res_corners = corner_list(global_cells(resident_cell, res_block // N_COL, res_block % N_COL), resident_corner, resident_frac)
    mig_block = (jnp.arange(MIGRANTS, dtype=jnp.int32) // MIG_DEV).astype(jnp.int32)
    mig_row = mig_block // N_COL
    mig_source = mig_block % N_COL
    destination = migrant_dest[:, 0]
    mig_corners = corner_list(global_cells(migrant_cell, mig_row, destination), migrant_corner, migrant_frac)

    extended = jnp.zeros(((NG + 2) ** 3,), jnp.float32)
    for flat_index, weight in res_corners:
        extended = extended.at[flat_index].add(resident_charge * weight)
    for flat_index, weight in mig_corners:
        extended = extended.at[flat_index].add(migrant_charge * weight)
    charge = extended.reshape(NG + 2, NG + 2, NG + 2)[1:-1, 1:-1, 1:-1]
    padded = jnp.zeros((MG, MG, MG), jnp.float32).at[:NG, :NG, :NG].set(charge)
    spectrum = jnp.fft.fftn(padded)

    position = jnp.arange(MG, dtype=jnp.int32)
    half_pos = position // 2
    wave_of = jnp.where(position % 2 == 0, half_pos, jnp.where(half_pos == 0, MG // 2, MG - half_pos)).astype(jnp.int32)

    fields = []
    for channel in range(3):
        kernel_real = jnp.zeros((MG, MG, MG), jnp.float32).at[wave_of].set(green[channel, 0].astype(jnp.float32))
        kernel_imag = jnp.zeros((MG, MG, MG), jnp.float32).at[wave_of].set(green[channel, 1].astype(jnp.float32))
        kernel = jnp.transpose(kernel_real + 1j * kernel_imag, (1, 2, 0))
        field_real = jnp.real(jnp.fft.ifftn(spectrum * kernel))[:NG, :NG, :NG]
        fields.append(jnp.pad(field_real, 1).reshape(-1))

    res_values = jnp.stack([corner_sum(res_corners, fields[channel]) for channel in range(3)])
    resident_kicked = resident_momentum + resident_charge[None, :] * res_values
    mig_values = jnp.stack([corner_sum(mig_corners, fields[channel]) for channel in range(3)])
    mig_kicked = migrant_momentum + migrant_charge[None, :] * mig_values

    dest_blocks = destination.reshape(device_total, MIG_DEV)
    dest_hits = (dest_blocks[:, :, None] == jnp.arange(N_COL, dtype=jnp.int32)[None, None, :]).astype(jnp.int32)
    slot_rank = jnp.sum((jnp.cumsum(dest_hits, axis=1) - dest_hits) * dest_hits, axis=2).astype(jnp.int32).reshape(MIGRANTS)
    slot_index = ((mig_row * N_COL + destination) * (N_COL * CAP) + mig_source * CAP + slot_rank).astype(jnp.int32)
    migrant_kicked = jnp.zeros((3, SLOTS), jnp.float32).at[:, slot_index].set(mig_kicked)
    return (resident_kicked, migrant_kicked)
```

```python
import functools

import jax
import jax.numpy as jnp
import numpy as np
from jax import lax
from jax.experimental import pallas as pl
from jax.experimental.pallas import tpu as pltpu
from jax.sharding import PartitionSpec as P

F32, BF, I32 = jnp.float32, jnp.bfloat16, jnp.int32
N_ROW, N_COL = 4, 32
SLOTS = N_ROW * N_COL
ROWS = 208
PAD = 256
BIG = 48 << 20


def split_np(table):
    hi = table.astype(jnp.bfloat16)
    return hi, (table - hi.astype(np.float64)).astype(jnp.bfloat16)


def row_places():
    layer, y = np.full(PAD, -1), np.zeros(PAD, int)
    layer[:192], y[:192] = np.arange(192) // 32, np.arange(192) % 32
    for side in range(2):
        layer[192 + 8 * side : 198 + 8 * side] = np.arange(6)
        y[192 + 8 * side : 200 + 8 * side] = 33 * side - 1
    return layer, y


def tables():
    wave = np.arange(256)
    layer, y = row_places()
    yg = 32 * np.arange(N_ROW)[:, None] + y[None]
    live = ((layer >= 0)[None] & (yg >= 0) & (yg < 128)).reshape(-1, 1)
    angle = 2 * np.pi / 256 * (yg.reshape(-1, 1) * wave % 256)
    ey = np.concatenate([np.cos(angle), np.sin(angle)], axis=1) * live
    zg = (4 * np.arange(N_COL)[None] + np.arange(6)[:, None] - 1).reshape(-1)
    live = ((zg >= 0) & (zg < 128))[None]
    angle = 2 * np.pi / 256 * (wave[:, None] * zg % 256)
    ez = np.stack([np.cos(angle) * live, np.sin(angle) * live])
    ezt = ez.transpose(0, 2, 1).reshape(384, 256)
    x, j = np.arange(128), np.arange(128)
    angle = 2 * np.pi / 256 * (j[:, None] * x % 256)
    imag = -np.sin(angle)
    imag[0] = 1 - 2 * (x % 2)
    dx = np.concatenate([np.cos(angle), imag])
    return [split_np(t) for t in (ey, ez.reshape(512, 192), ezt, dx, dx.T / 256.0**3)]


def split(v):
    hi = v.astype(BF)
    return hi, (v - hi.astype(F32)).astype(BF)


def dot3(a, b, dims=((1,), (0,))):
    one = lambda p, q: lax.dot_general(p, q, (dims, ((), ())), preferred_element_type=F32)
    return one(a[0], b[0]) + (one(a[0], b[1]) + one(a[1], b[0]))


def tile16(row, n):
    return jnp.broadcast_to(row, (16, n)).astype(BF)


def yz_weights(cell, corner, fy, fz, q, n, write):
    y = (cell >> 7) & 31
    z = (cell >> 12) + 1
    yfar = y + ((corner >> 1) & 1) * 2 - 1
    zfar = z + ((corner >> 2) & 1) * 2 - 1
    io8 = lax.broadcasted_iota(I32, (8, n), 0)
    wz = jnp.where(io8 == z, (1.0 - fz) * q, jnp.where(io8 == zfar, fz * q, 0.0))
    near = wz * (1.0 - fy)
    far = wz * fy
    nh = near.astype(BF).astype(F32); nl = near - nh
    fh = far.astype(BF).astype(F32); fl = far - fh
    io16 = lax.broadcasted_iota(I32, (16, n), 0).astype(BF)
    yb = jnp.broadcast_to(y.astype(F32), (16, n)).astype(BF)
    yfb = jnp.broadcast_to(yfar.astype(F32), (16, n)).astype(BF)
    zero = jnp.zeros((16, n), BF)
    masks = [(yb == io16, yfb == io16), (yb == io16 + 16.0, yfb == io16 + 16.0)]
    for ze in range(6):
        a, b, c, d = (tile16(v[ze:ze+1], n) for v in (nh, fh, nl, fl))
        for h in range(2):
            mn, mf = masks[h]
            write(ze*32 + h*16, jnp.where(mn, a, jnp.where(mf, b, zero)), jnp.where(mn, c, jnp.where(mf, d, zero)))
    isb = yfar < 0
    isa = yfar > 31
    rh = jnp.concatenate([jnp.where(isb, fh, 0.0), jnp.where(isa, fh, 0.0)], axis=0).astype(BF)
    rl = jnp.concatenate([jnp.where(isb, fl, 0.0), jnp.where(isa, fl, 0.0)], axis=0).astype(BF)
    write(192, rh, rl)

def deposit_kernel(cell_ref, corner_ref, frac_ref, q_ref, out_ref, a_ref, b_ref, *, n):
    @pl.when(pl.program_id(0) == 0)
    def _():
        out_ref[...] = jnp.zeros_like(out_ref)
    total = cell_ref.shape[-1]
    for s in range(total // n):
        sl = pl.ds(s*n, n)
        cell = cell_ref[:, sl]; corner = corner_ref[:, sl]; q = q_ref[:, sl]
        fx = frac_ref[0:1, sl]; fy = frac_ref[1:2, sl]; fz = frac_ref[2:3, sl]
        def write(r, hi, lo):
            a_ref[r:r+16, sl] = hi
            a_ref[ROWS+r:ROWS+r+16, sl] = lo
        yz_weights(cell, corner, fy, fz, q, n, write)
        x = cell & 127
        xfar = x + (corner & 1)*2 - 1
        gx = 1.0 - fx
        gh = gx.astype(BF).astype(F32); gl = gx - gh
        fh = fx.astype(BF).astype(F32); fl = fx - fh
        io16 = lax.broadcasted_iota(I32, (16, n), 0).astype(BF)
        xb = tile16(x.astype(F32), n); xfb = tile16(xfar.astype(F32), n)
        gh, gl, fh, fl = (tile16(v, n) for v in (gh, gl, fh, fl))
        zero = jnp.zeros((16, n), BF)
        for t in range(8):
            mn = xb == io16 + BF(16*t); mf = xfb == io16 + BF(16*t)
            b_ref[16*t:16*t+16, sl] = jnp.where(mn, gh, jnp.where(mf, fh, zero))
            b_ref[128+16*t:128+16*t+16, sl] = jnp.where(mn, gl, jnp.where(mf, fl, zero))
    out_ref[...] += lax.dot_general(a_ref[...], b_ref[...], (((1,),(1,)),((),())), preferred_element_type=F32)

def deposit(cell, corner, frac, q, blk=2048, n=512):
    total = cell.shape[-1]
    row = pl.BlockSpec((1, blk), lambda i: (0, i))
    return pl.pallas_call(
        functools.partial(deposit_kernel, n=n),
        out_shape=jax.ShapeDtypeStruct((2*ROWS, 256), F32),
        grid=(total//blk,),
        in_specs=[row, row, pl.BlockSpec((3, blk), lambda i: (0, i)), row],
        out_specs=pl.BlockSpec((2*ROWS, 256), lambda i: (0, 0)),
        scratch_shapes=[pltpu.VMEM((2*ROWS, blk), BF), pltpu.VMEM((256, blk), BF)],
        compiler_params=pltpu.CompilerParams(vmem_limit_bytes=48 << 20),
    )(cell.reshape(1, -1), corner.reshape(1, -1), frac, q.reshape(1, -1))

def kick_kernel(ft_ref, cell_ref, corner_ref, frac_ref, q_ref, mom_ref, out_ref, w_ref, *, n):
    total = cell_ref.shape[-1]
    for s in range(total // n):
        sl = pl.ds(s*n, n)
        cell = cell_ref[:, sl]; corner = corner_ref[:, sl]; q = q_ref[:, sl]
        fx = frac_ref[0:1, sl]; fy = frac_ref[1:2, sl]; fz = frac_ref[2:3, sl]
        def write(r, hi, lo):
            w_ref[r:r+16, sl] = hi
            w_ref[ROWS+r:ROWS+r+16, sl] = hi
            w_ref[2*ROWS+r:2*ROWS+r+16, sl] = lo
        yz_weights(cell, corner, fy, fz, q, n, write)
        y = jnp.dot(ft_ref[...], w_ref[:, sl], preferred_element_type=F32)
        x = cell & 127
        xfar = x + (corner & 1)*2 - 1
        io = lax.broadcasted_iota(I32, (128, n), 0)
        wx = jnp.where(io == x, 1.0 - fx, jnp.where(io == xfar, fx, 0.0))
        for a in range(3):
            out_ref[a:a+1, sl] = mom_ref[a:a+1, sl] + jnp.sum(y[a*128:(a+1)*128] * wx, axis=0, keepdims=True)

def kick(ft, cell, corner, frac, q, mom, blk=2048, n=512):
    total = cell.shape[-1]
    row = pl.BlockSpec((1, blk), lambda i: (0, i))
    r3 = pl.BlockSpec((3, blk), lambda i: (0, i))
    return pl.pallas_call(
        functools.partial(kick_kernel, n=n),
        out_shape=jax.ShapeDtypeStruct((3, total), F32),
        grid=(total//blk,),
        in_specs=[pl.BlockSpec(ft.shape, lambda i: (0, 0)), row, row, r3, row, r3],
        out_specs=r3,
        scratch_shapes=[pltpu.VMEM((3*ROWS, blk), BF)],
        compiler_params=pltpu.CompilerParams(vmem_limit_bytes=48 << 20),
    )(ft, cell.reshape(1, -1), corner.reshape(1, -1), frac, q.reshape(1, -1), mom)


def pack_kernel(dest_ref, cell_ref, corner_ref, frac_ref, q_ref, mom_ref, out_ref, lhs_ref):
    total = dest_ref.shape[-1]
    dest = dest_ref[...]
    hits = (lax.broadcasted_iota(I32, (N_COL, total), 0) == dest).astype(F32)
    upper = (lax.broadcasted_iota(I32, (256, 256), 0) < lax.broadcasted_iota(I32, (256, 256), 1)).astype(BF)
    carry = jnp.zeros((N_COL, 1), F32)
    ranks = []
    for s in range(0, total, 256):
        part = hits[:, s : s + 256]
        before = jnp.dot(part.astype(BF), upper, preferred_element_type=F32) + carry
        carry = carry + jnp.sum(part, axis=1, keepdims=True)
        ranks.append(jnp.sum(part * before, axis=0, keepdims=True))
    rank = jnp.concatenate(ranks, axis=1)
    cap = out_ref.shape[-1]
    choose = (lax.broadcasted_iota(I32, (cap, total), 0).astype(F32) == rank).astype(BF)
    payload = jnp.concatenate(
        [
            frac_ref[...],
            q_ref[...],
            mom_ref[...],
            cell_ref[...].astype(F32),
            corner_ref[...].astype(F32),
            jnp.zeros((7, total), F32),
        ],
        axis=0,
    )
    hi = payload.astype(BF)
    rest = payload - hi.astype(F32)
    mid = rest.astype(BF)
    low = (rest - mid.astype(F32)).astype(BF)
    destb = tile16(dest.astype(F32), total)
    zero = jnp.zeros((16, total), BF)
    for d in range(N_COL):
        mask = destb == BF(d)
        for i, piece in enumerate((hi, mid, low)):
            lhs_ref[i * 512 + d * 16 : i * 512 + d * 16 + 16] = jnp.where(mask, piece, zero)
    got = lax.dot_general(lhs_ref[...], choose, (((1,), (1,)), ((), ())), preferred_element_type=F32)
    got = (got[:512] + got[512:1024]) + got[1024:]
    for d in range(N_COL):
        out_ref[d] = got[d * 16 : d * 16 + 9]


def pack(dest, cell, corner, frac, q, mom):
    total = cell.shape[0]
    cap = 2 * total // N_COL
    return pl.pallas_call(
        pack_kernel,
        name="pack",
        out_shape=jax.ShapeDtypeStruct((N_COL, 9, cap), F32),
        scratch_shapes=[pltpu.VMEM((3 * 512, total), BF)],
        compiler_params=pltpu.CompilerParams(vmem_limit_bytes=BIG),
    )(dest.reshape(1, -1), cell.reshape(1, -1), corner.reshape(1, -1), frac, q.reshape(1, -1), mom)


def spread_kernel(first_ref, second_ref, dxh_ref, dxl_ref, out_ref):
    acc = first_ref[...] + second_ref[...]
    grid = (acc[:ROWS, :128] + acc[ROWS:, 128:]) + (acc[:ROWS, 128:] + acc[ROWS:, :128])
    sent = dot3((dxh_ref[...], dxl_ref[...]), split(grid), ((1,), (1,)))
    sent = jnp.concatenate([sent, jnp.zeros((256, PAD - ROWS), F32)], axis=1)
    for part in range(2):
        for half in range(2):
            out_ref[:, 2 * part + half, :] = sent[128 * part : 128 * part + 128, 128 * half : 128 * half + 128]


def spread(first, second, dx):
    return pl.pallas_call(
        spread_kernel,
        name="spread",
        out_shape=jax.ShapeDtypeStruct((SLOTS, 4, 128), F32),
        compiler_params=pltpu.CompilerParams(vmem_limit_bytes=BIG),
    )(first, second, *dx)


def layer_of(shape):
    lane = lax.broadcasted_iota(I32, shape, 1)
    return jnp.where(lane < 192, lane // 32, jnp.where(lane < ROWS, lane % 8, 6))


def solve_kernel(got_ref, green_ref, eyh_ref, eyl_ref, ezh_ref, ezl_ref, zth_ref, ztl_ref, out_ref, lhs_ref, s_ref, q_ref):
    first = (lax.axis_index("row") == 0) & (lax.axis_index("col") == 0)
    layer = layer_of((N_COL, PAD))
    ey = (eyh_ref, eyl_ref)

    @pl.when(pl.program_id(0) == 0)
    def _():
        for part in range(2):
            for r in range(N_ROW):
                rows = slice(32 * r, 32 * r + 32)
                both = jnp.concatenate([got_ref[rows, 2 * part, :], got_ref[rows, 2 * part + 1, :]], axis=1)
                for ze in range(6):
                    hi, lo = split(jnp.where(layer == ze, both, 0.0))
                    where = slice(192 * part + 32 * ze, 192 * part + 32 * ze + 32)
                    lhs_ref[0, where, PAD * r : PAD * r + PAD] = hi
                    lhs_ref[1, where, PAD * r : PAD * r + PAD] = lo
        u = dot3((lhs_ref[0], lhs_ref[1]), (eyh_ref[...], eyl_ref[...]))
        re_c, re_s, im_c, im_s = u[:192, :256], u[:192, 256:], u[192:, :256], u[192:, 256:]
        ez = (ezh_ref[...], ezl_ref[...])

        def forward(real, imag):
            v = dot3(ez, split(jnp.concatenate([real, imag], axis=1)))
            return v[:256, :256] + v[256:, 256:], v[:256, 256:] - v[256:, :256]

        @pl.when(first)
        def _():
            s_ref[0], s_ref[1] = forward(re_c, -re_s)
            s_ref[2], s_ref[3] = forward(im_c, -im_s)

        @pl.when(jnp.logical_not(first))
        def _():
            s_ref[0], s_ref[1] = forward(re_c + im_s, im_c - re_s)

    index = lax.broadcasted_iota(I32, (256, 256), 0) + lax.broadcasted_iota(I32, (256, 256), 1)
    mirror = ((index == 0) | (index == 256)).astype(BF)

    def flip(plane):
        half = jnp.dot(mirror, plane, preferred_element_type=F32).astype(BF)
        return jnp.dot(half, mirror, preferred_element_type=F32)

    def at(part, sign):
        return green_ref[0, part, sign]

    @pl.when(first)
    def _():
        real0 = 0.5 * (at(0, 0).astype(F32) + flip(at(0, 0)))
        imag0 = 0.5 * (at(1, 0).astype(F32) - flip(at(1, 0)))
        real1 = 0.5 * (at(0, 1).astype(F32) + flip(at(0, 1)))
        imag1 = 0.5 * (at(1, 1).astype(F32) - flip(at(1, 1)))
        a_re = s_ref[0] * real0 - s_ref[1] * imag0
        a_im = s_ref[0] * imag0 + s_ref[1] * real0
        b_re = s_ref[2] * real1 - s_ref[3] * imag1
        b_im = s_ref[2] * imag1 + s_ref[3] * real1
        q_ref[0], q_ref[1] = a_re - b_im, a_im + b_re

    @pl.when(jnp.logical_not(first))
    def _():
        real = at(0, 0).astype(F32) + flip(at(0, 1))
        imag = at(1, 0).astype(F32) - flip(at(1, 1))
        q_ref[0] = s_ref[0] * real - s_ref[1] * imag
        q_ref[1] = s_ref[0] * imag + s_ref[1] * real

    q = split(jnp.concatenate([q_ref[0], q_ref[1]], axis=1))
    v = dot3((zth_ref[...], ztl_ref[...]), q)
    v = jnp.concatenate([v[:192, :256] - v[192:, 256:], v[:192, 256:] + v[192:, :256]], axis=0)
    v = split(v)
    for r in range(N_ROW):
        rows = slice(PAD * r, PAD * r + PAD)
        cos = dot3(v, (eyh_ref[rows, :256], eyl_ref[rows, :256]), ((1,), (1,)))
        sin = dot3(v, (eyh_ref[rows, 256:], eyl_ref[rows, 256:]), ((1,), (1,)))
        w = (cos[:192] - sin[192:], cos[192:] + sin[:192])
        for part in range(2):
            mine = jnp.zeros((N_COL, PAD), F32)
            for ze in range(6):
                mine = jnp.where(layer == ze, w[part][32 * ze : 32 * ze + 32], mine)
            for half in range(2):
                out_ref[32 * r : 32 * r + 32, 0, 2 * part + half, :] = mine[:, 128 * half : 128 * half + 128]


def solve(got, green, ey, ez, ezt):
    whole = lambda a: pl.BlockSpec(a.shape, lambda i: (0,) * a.ndim)
    consts = [*ey, *ez, *ezt]
    return pl.pallas_call(
        solve_kernel,
        name="solve",
        out_shape=jax.ShapeDtypeStruct((SLOTS, 3, 4, 128), F32),
        grid=(3,),
        in_specs=[whole(got), pl.BlockSpec((1, 2, 2, 256, 256), lambda i: (i, 0, 0, 0, 0)), *map(whole, consts)],
        out_specs=pl.BlockSpec((SLOTS, 1, 4, 128), lambda i: (0, i, 0, 0)),
        scratch_shapes=[pltpu.VMEM((2, 384, 1024), BF), pltpu.VMEM((4, 256, 256), F32), pltpu.VMEM((2, 256, 256), F32)],
        compiler_params=pltpu.CompilerParams(vmem_limit_bytes=BIG),
    )(got, green, *consts)


def table_kernel(got_ref, xih_ref, xil_ref, out_ref):
    for a in range(3):
        parts = [
            jnp.concatenate([got_ref[:, a, 2 * part, :], got_ref[:, a, 2 * part + 1, :]], axis=1) for part in range(2)
        ]
        field = dot3((xih_ref[...], xil_ref[...]), split(jnp.concatenate(parts, axis=0)))
        hi, lo = split(field[:, :ROWS])
        out_ref[128 * a : 128 * a + 128] = jnp.concatenate([hi, lo, hi], axis=1)


def table(got, xi):
    return pl.pallas_call(
        table_kernel,
        name="table",
        out_shape=jax.ShapeDtypeStruct((384, 3 * ROWS), BF),
        compiler_params=pltpu.CompilerParams(vmem_limit_bytes=BIG),
    )(got, *xi)


def body(
    resident_cell,
    resident_corner,
    resident_frac,
    resident_charge,
    resident_momentum,
    migrant_dest,
    migrant_cell,
    migrant_corner,
    migrant_frac,
    migrant_charge,
    migrant_momentum,
    green,
):
    ey, ez, ezt, dx, xi = [tuple(map(jnp.asarray, pair)) for pair in tables()]
    packed = pack(
        migrant_dest.reshape(-1), migrant_cell, migrant_corner, migrant_frac, migrant_charge, migrant_momentum
    )
    arrived = lax.all_to_all(packed, "col", 0, 0, tiled=True)
    arrived = arrived.transpose(1, 0, 2).reshape(9, -1)
    moved = (arrived[7].astype(I32), arrived[8].astype(I32), arrived[0:3], arrived[3])
    stayed = (resident_cell, resident_corner, resident_frac, resident_charge)
    sent = spread(deposit(*stayed), deposit(*moved), dx)
    got = lax.all_to_all(sent, ("row", "col"), 0, 0, tiled=True)
    sent = solve(got, green, ey, ez, ezt)
    got = lax.all_to_all(sent, ("row", "col"), 0, 0, tiled=True)
    field = table(got, xi)
    return kick(field, *stayed, resident_momentum), kick(field, *moved, arrived[4:7])


def solution(mesh):
    both = ("row", "col")
    in_specs = (
        P(both),
        P(both),
        P(None, both),
        P(both),
        P(None, both),
        P(both, None),
        P(both),
        P(both),
        P(None, both),
        P(both),
        P(None, both),
        P(None, None, both, None, None),
    )
    out_specs = (P(None, both), P(None, both))
    return jax.shard_map(body, mesh=mesh, in_specs=in_specs, out_specs=out_specs, check_vma=False)
```

```python
import functools

import jax
import jax.numpy as jnp
import numpy as np
from jax import lax
from jax.experimental import pallas as pl
from jax.experimental.pallas import tpu as pltpu
from jax.sharding import PartitionSpec as P

F32, BF, I32 = jnp.float32, jnp.bfloat16, jnp.int32
N_ROW, N_COL = 4, 32
SLOTS = N_ROW * N_COL
ROWS = 208
PAD = 256
BIG = 48 << 20


def split_np(table):
    hi = table.astype(jnp.bfloat16)
    return hi, (table - hi.astype(np.float64)).astype(jnp.bfloat16)


def row_places():
    layer, y = np.full(PAD, -1), np.zeros(PAD, int)
    layer[:192], y[:192] = np.arange(192) // 32, np.arange(192) % 32
    for side in range(2):
        layer[192 + 8 * side : 198 + 8 * side] = np.arange(6)
        y[192 + 8 * side : 200 + 8 * side] = 33 * side - 1
    return layer, y


def tables():
    wave = np.arange(256)
    layer, y = row_places()
    yg = 32 * np.arange(N_ROW)[:, None] + y[None]
    live = ((layer >= 0)[None] & (yg >= 0) & (yg < 128)).reshape(-1, 1)
    angle = 2 * np.pi / 256 * (yg.reshape(-1, 1) * wave % 256)
    ey = np.concatenate([np.cos(angle), np.sin(angle)], axis=1) * live
    zg = (4 * np.arange(N_COL)[None] + np.arange(6)[:, None] - 1).reshape(-1)
    live = ((zg >= 0) & (zg < 128))[None]
    angle = 2 * np.pi / 256 * (wave[:, None] * zg % 256)
    ez = np.stack([np.cos(angle) * live, np.sin(angle) * live])
    ezt = ez.transpose(0, 2, 1).reshape(384, 256)
    x, j = np.arange(128), np.arange(128)
    angle = 2 * np.pi / 256 * (j[:, None] * x % 256)
    imag = -np.sin(angle)
    imag[0] = 1 - 2 * (x % 2)
    dx = np.concatenate([np.cos(angle), imag])
    return [split_np(t) for t in (ey, ez.reshape(512, 192), ezt, dx, dx.T / 256.0**3)]


def split(v):
    hi = v.astype(BF)
    return hi, (v - hi.astype(F32)).astype(BF)


def dot3(a, b, dims=((1,), (0,))):
    one = lambda p, q: lax.dot_general(p, q, (dims, ((), ())), preferred_element_type=F32)
    return one(a[0], b[0]) + (one(a[0], b[1]) + one(a[1], b[0]))


def tile16(row, n):
    return jnp.broadcast_to(row, (16, n)).astype(BF)


def yz_weights(cell, corner, fy, fz, q, n, write):
    y = (cell >> 7) & 31
    z = (cell >> 12) + 1
    yfar = y + ((corner >> 1) & 1) * 2 - 1
    zfar = z + ((corner >> 2) & 1) * 2 - 1
    io8 = lax.broadcasted_iota(I32, (8, n), 0)
    wz = jnp.where(io8 == z, (1.0 - fz) * q, jnp.where(io8 == zfar, fz * q, 0.0))
    near = wz * (1.0 - fy)
    far = wz * fy
    nh = near.astype(BF).astype(F32); nl = near - nh
    fh = far.astype(BF).astype(F32); fl = far - fh
    io16 = lax.broadcasted_iota(I32, (16, n), 0).astype(BF)
    yb = jnp.broadcast_to(y.astype(F32), (16, n)).astype(BF)
    yfb = jnp.broadcast_to(yfar.astype(F32), (16, n)).astype(BF)
    zero = jnp.zeros((16, n), BF)
    masks = [(yb == io16, yfb == io16), (yb == io16 + 16.0, yfb == io16 + 16.0)]
    for ze in range(6):
        a, b, c, d = (tile16(v[ze:ze+1], n) for v in (nh, fh, nl, fl))
        for h in range(2):
            mn, mf = masks[h]
            write(ze*32 + h*16, jnp.where(mn, a, jnp.where(mf, b, zero)), jnp.where(mn, c, jnp.where(mf, d, zero)))
    isb = yfar < 0
    isa = yfar > 31
    rh = jnp.concatenate([jnp.where(isb, fh, 0.0), jnp.where(isa, fh, 0.0)], axis=0).astype(BF)
    rl = jnp.concatenate([jnp.where(isb, fl, 0.0), jnp.where(isa, fl, 0.0)], axis=0).astype(BF)
    write(192, rh, rl)

def x_weights(cell, corner, fx, n, write):
    x = cell & 127
    xfar = x + (corner & 1) * 2 - 1
    gx = 1.0 - fx
    gh = gx.astype(BF).astype(F32)
    fh = fx.astype(BF).astype(F32)
    gh, gl, fh, fl = (tile16(v, n) for v in (gh, gx - gh, fh, fx - fh))
    io16 = lax.broadcasted_iota(I32, (16, n), 0).astype(BF)
    xb, xfb = tile16(x.astype(F32), n), tile16(xfar.astype(F32), n)
    zero = jnp.zeros((16, n), BF)
    for t in range(8):
        near, far = xb == io16 + BF(16 * t), xfb == io16 + BF(16 * t)
        write(16 * t, jnp.where(near, gh, jnp.where(far, fh, zero)), jnp.where(near, gl, jnp.where(far, fl, zero)))


def deposit_block(rows, a_ref, b_ref, acc_ref, n):
    for s in range(a_ref.shape[1] // n):
        here = pl.ds(s * n, n)
        cell, corner, fx, fy, fz, q = rows(s)

        def write_a(r, hi, lo):
            a_ref[r : r + 16, here] = hi
            a_ref[ROWS + r : ROWS + r + 16, here] = lo

        def write_b(r, hi, lo):
            b_ref[r : r + 16, here] = hi
            b_ref[128 + r : 128 + r + 16, here] = lo

        yz_weights(cell, corner, fy, fz, q, n, write_a)
        x_weights(cell, corner, fx, n, write_b)
    acc_ref[...] += lax.dot_general(a_ref[...], b_ref[...], (((1,), (1,)), ((), ())), preferred_element_type=F32)


def pack_into(dest_ref, cell_ref, corner_ref, frac_ref, q_ref, mom_ref, lhs_ref, out_ref):
    total = dest_ref.shape[-1]
    dest = dest_ref[...]
    hits = (lax.broadcasted_iota(I32, (N_COL, total), 0) == dest).astype(F32)
    upper = (lax.broadcasted_iota(I32, (256, 256), 0) < lax.broadcasted_iota(I32, (256, 256), 1)).astype(BF)
    carry = jnp.zeros((N_COL, 1), F32)
    ranks = []
    for s in range(0, total, 256):
        part = hits[:, s : s + 256]
        before = jnp.dot(part.astype(BF), upper, preferred_element_type=F32) + carry
        carry = carry + jnp.sum(part, axis=1, keepdims=True)
        ranks.append(jnp.sum(part * before, axis=0, keepdims=True))
    rank = jnp.concatenate(ranks, axis=1)
    cap = out_ref.shape[-1]
    choose = (lax.broadcasted_iota(I32, (cap, total), 0).astype(F32) == rank).astype(BF)
    payload = jnp.concatenate(
        [
            frac_ref[...],
            q_ref[...],
            mom_ref[...],
            cell_ref[...].astype(F32),
            corner_ref[...].astype(F32),
            jnp.zeros((7, total), F32),
        ],
        axis=0,
    )
    hi = payload.astype(BF)
    rest = payload - hi.astype(F32)
    mid = rest.astype(BF)
    low = (rest - mid.astype(F32)).astype(BF)
    destb = tile16(dest.astype(F32), total)
    zero = jnp.zeros((16, total), BF)
    for d in range(N_COL):
        mask = destb == BF(d)
        for i, piece in enumerate((hi, mid, low)):
            lhs_ref[i * 512 + d * 16 : i * 512 + d * 16 + 16] = jnp.where(mask, piece, zero)
    got = lax.dot_general(lhs_ref[...], choose, (((1,), (1,)), ((), ())), preferred_element_type=F32)
    got = (got[:512] + got[512:1024]) + got[1024:]
    for d in range(N_COL):
        out_ref[d] = got[d * 16 : d * 16 + 9]


def kick_kernel(ft_ref, cell_ref, corner_ref, frac_ref, q_ref, mom_ref, out_ref, w_ref, *, n):
    total = cell_ref.shape[-1]
    for s in range(total // n):
        sl = pl.ds(s*n, n)
        cell = cell_ref[:, sl]; corner = corner_ref[:, sl]; q = q_ref[:, sl]
        fx = frac_ref[0:1, sl]; fy = frac_ref[1:2, sl]; fz = frac_ref[2:3, sl]
        def write(r, hi, lo):
            w_ref[r:r+16, sl] = hi
            w_ref[ROWS+r:ROWS+r+16, sl] = hi
            w_ref[2*ROWS+r:2*ROWS+r+16, sl] = lo
        yz_weights(cell, corner, fy, fz, q, n, write)
        y = jnp.dot(ft_ref[...], w_ref[:, sl], preferred_element_type=F32)
        x = cell & 127
        xfar = x + (corner & 1)*2 - 1
        io = lax.broadcasted_iota(I32, (128, n), 0)
        wx = jnp.where(io == x, 1.0 - fx, jnp.where(io == xfar, fx, 0.0))
        for a in range(3):
            out_ref[a:a+1, sl] = mom_ref[a:a+1, sl] + jnp.sum(y[a*128:(a+1)*128] * wx, axis=0, keepdims=True)

def kick(ft, cell, corner, frac, q, mom, blk=2048, n=512):
    total = cell.shape[-1]
    row = pl.BlockSpec((1, blk), lambda i: (0, i))
    r3 = pl.BlockSpec((3, blk), lambda i: (0, i))
    return pl.pallas_call(
        functools.partial(kick_kernel, n=n),
        out_shape=jax.ShapeDtypeStruct((3, total), F32),
        grid=(total//blk,),
        in_specs=[pl.BlockSpec(ft.shape, lambda i: (0, 0)), row, row, r3, row, r3],
        out_specs=r3,
        scratch_shapes=[pltpu.VMEM((3*ROWS, blk), BF)],
        compiler_params=pltpu.CompilerParams(vmem_limit_bytes=48 << 20),
    )(ft, cell.reshape(1, -1), corner.reshape(1, -1), frac, q.reshape(1, -1), mom)


def layer_of(shape):
    lane = lax.broadcasted_iota(I32, shape, 1)
    return jnp.where(lane < 192, lane // 32, jnp.where(lane < ROWS, lane % 8, 6))


def green_into(green_ref, h_ref, first):
    index = lax.broadcasted_iota(I32, (256, 256), 0) + lax.broadcasted_iota(I32, (256, 256), 1)
    mirror = ((index == 0) | (index == 256)).astype(BF)

    def flip(plane):
        half = jnp.dot(mirror, plane, preferred_element_type=F32).astype(BF)
        return jnp.dot(half, mirror, preferred_element_type=F32)

    @pl.when(first)
    def _():
        for a in range(3):
            for sign in range(2):
                real, imag = green_ref[a, 0, sign], green_ref[a, 1, sign]
                h_ref[a, 2 * sign] = 0.5 * (real.astype(F32) + flip(real))
                h_ref[a, 2 * sign + 1] = 0.5 * (imag.astype(F32) - flip(imag))

    @pl.when(jnp.logical_not(first))
    def _():
        for a in range(3):
            h_ref[a, 0] = green_ref[a, 0, 0].astype(F32) + flip(green_ref[a, 0, 1])
            h_ref[a, 1] = green_ref[a, 1, 0].astype(F32) - flip(green_ref[a, 1, 1])


def forward_into(got_ref, ey, ez, lhs_ref, s_ref, first):
    layer = layer_of((N_COL, PAD))
    for part in range(2):
        for r in range(N_ROW):
            rows = slice(32 * r, 32 * r + 32)
            both = jnp.concatenate([got_ref[rows, 2 * part, :], got_ref[rows, 2 * part + 1, :]], axis=1)
            for ze in range(6):
                hi, lo = split(jnp.where(layer == ze, both, 0.0))
                where = slice(192 * part + 32 * ze, 192 * part + 32 * ze + 32)
                lhs_ref[0, where, PAD * r : PAD * r + PAD] = hi
                lhs_ref[1, where, PAD * r : PAD * r + PAD] = lo
    u = dot3((lhs_ref[0], lhs_ref[1]), (ey[0][...], ey[1][...]))
    re_c, re_s, im_c, im_s = u[:192, :256], u[:192, 256:], u[192:, :256], u[192:, 256:]
    ezs = (ez[0][...], ez[1][...])

    def forward(real, imag):
        v = dot3(ezs, split(jnp.concatenate([real, imag], axis=1)))
        return v[:256, :256] + v[256:, 256:], v[:256, 256:] - v[256:, :256]

    @pl.when(first)
    def _():
        s_ref[0], s_ref[1] = forward(re_c, -re_s)
        s_ref[2], s_ref[3] = forward(im_c, -im_s)

    @pl.when(jnp.logical_not(first))
    def _():
        s_ref[0], s_ref[1] = forward(re_c + im_s, im_c - re_s)


def back_into(a, h_ref, s_ref, q_ref, zt, ey, out_ref, first):
    layer = layer_of((N_COL, PAD))
    a_re = s_ref[0] * h_ref[a, 0] - s_ref[1] * h_ref[a, 1]
    a_im = s_ref[0] * h_ref[a, 1] + s_ref[1] * h_ref[a, 0]
    q_ref[0], q_ref[1] = a_re, a_im

    @pl.when(first)
    def _():
        b_re = s_ref[2] * h_ref[a, 2] - s_ref[3] * h_ref[a, 3]
        b_im = s_ref[2] * h_ref[a, 3] + s_ref[3] * h_ref[a, 2]
        q_ref[0] = q_ref[0] - b_im
        q_ref[1] = q_ref[1] + b_re

    q = split(jnp.concatenate([q_ref[0], q_ref[1]], axis=1))
    v = dot3((zt[0][...], zt[1][...]), q)
    v = jnp.concatenate([v[:192, :256] - v[192:, 256:], v[:192, 256:] + v[192:, :256]], axis=0)
    v = split(v)
    for r in range(N_ROW):
        rows = slice(PAD * r, PAD * r + PAD)
        cos = dot3(v, (ey[0][rows, :256], ey[1][rows, :256]), ((1,), (1,)))
        sin = dot3(v, (ey[0][rows, 256:], ey[1][rows, 256:]), ((1,), (1,)))
        w = (cos[:192] - sin[192:], cos[192:] + sin[:192])
        for part in range(2):
            mine = jnp.zeros((N_COL, PAD), F32)
            for ze in range(6):
                mine = jnp.where(layer == ze, w[part][32 * ze : 32 * ze + 32], mine)
            for half in range(2):
                out_ref[a, 32 * r : 32 * r + 32, 2 * part + half, :] = mine[:, 128 * half : 128 * half + 128]


MESH = pl.DeviceIdType.MESH
N_IN = 21


def field_kernel(*refs, n):
    hbm, (table_ref, moved_ref) = refs[:N_IN], refs[N_IN : N_IN + 2]
    held = refs[N_IN + 2 : 2 * N_IN + 2]
    (lhs_p, pack_s, pack_r, a_ref, b_ref, acc_ref, send1, recv1, h_ref, lhs_f, s_ref, q_ref, send2, recv2) = refs[
        2 * N_IN + 2 : 2 * N_IN + 16
    ]
    in_sem, own_sem, ss_m, rs_m, ss_1, rs_1, ss_2, rs_2 = refs[2 * N_IN + 16 :]
    row, col = lax.axis_index("row"), lax.axis_index("col")
    me = row * N_COL + col
    first = me == 0

    def device(d):
        return (d >> 5, d & 31)

    copies = [pltpu.make_async_copy(h, v, in_sem.at[i]) for i, (h, v) in enumerate(zip(hbm, held))]
    for copy in copies:
        copy.start()

    barrier = pltpu.get_barrier_semaphore()

    def greet(i, _):
        pl.semaphore_signal(barrier, inc=1, device_id=device((me + i) & 127), device_id_type=MESH)
        return 0

    lax.fori_loop(1, SLOTS, greet, 0)
    acc_ref[...] = jnp.zeros_like(acc_ref)

    for copy in copies[:6]:
        copy.wait()
    pack_into(*held[:6], lhs_p, pack_s)
    for copy in copies[6:10]:
        copy.wait()
    cell_ref, corner_ref, frac_ref, q_in = held[6:10]
    blk = a_ref.shape[1]
    steps = cell_ref.shape[1] // blk

    def resident(i, _):
        def rows(s):
            here = pl.ds(pl.multiple_of(i * blk + s * n, n), n)
            return (
                cell_ref[:, here],
                corner_ref[:, here],
                frac_ref[0:1, here],
                frac_ref[1:2, here],
                frac_ref[2:3, here],
                q_in[:, here],
            )

        deposit_block(rows, a_ref, b_ref, acc_ref, n)
        return 0

    lax.fori_loop(0, steps // 2, resident, 0)
    pl.semaphore_wait(barrier, SLOTS - 1)

    def send_migrants(i, _):
        c = (col + i) & 31
        pltpu.make_async_remote_copy(
            src_ref=pack_s.at[c],
            dst_ref=pack_r.at[col],
            send_sem=ss_m,
            recv_sem=rs_m,
            device_id=(row, c),
            device_id_type=MESH,
        ).start()
        return 0

    lax.fori_loop(1, N_COL, send_migrants, 0)
    own = pltpu.make_async_copy(pack_s.at[col], pack_r.at[col], own_sem.at[0])
    own.start()
    lax.fori_loop(steps // 2, steps, resident, 0)
    own.wait()
    rest = pl.ds(0, N_COL - 1)
    pltpu.make_async_remote_copy(
        src_ref=pack_s.at[rest],
        dst_ref=pack_r.at[rest],
        send_sem=ss_m,
        recv_sem=rs_m,
        device_id=(row, col),
        device_id_type=MESH,
    ).wait()
    for s in range(N_COL):
        moved_ref[:, 128 * s : 128 * s + 128] = pack_r[s]

    def migrant(i, _):
        def rows(s):
            here = pl.ds(pl.multiple_of(i * blk + s * n, n), n)
            got = moved_ref[:, here]
            return (
                got[7:8].astype(I32),
                got[8:9].astype(I32),
                got[0:1],
                got[1:2],
                got[2:3],
                got[3:4],
            )

        deposit_block(rows, a_ref, b_ref, acc_ref, n)
        return 0

    lax.fori_loop(0, moved_ref.shape[1] // blk, migrant, 0)
    for copy in copies[10:]:
        copy.wait()
    green_ref = held[10]
    ey, ez, zt, dx, xi = (held[11 + 2 * i : 13 + 2 * i] for i in range(5))

    acc = acc_ref[...]
    grid = (acc[:ROWS, :128] + acc[ROWS:, 128:]) + (acc[:ROWS, 128:] + acc[ROWS:, :128])
    sent = dot3((dx[0][...], dx[1][...]), split(grid), ((1,), (1,)))
    sent = jnp.concatenate([sent, jnp.zeros((256, PAD - ROWS), F32)], axis=1)
    for part in range(2):
        for half in range(2):
            send1[:, 2 * part + half, :] = sent[128 * part : 128 * part + 128, 128 * half : 128 * half + 128]

    def exchange(src, dst, ss, rs, own_at):
        def go(i, _):
            d = (me + i) & 127
            pltpu.make_async_remote_copy(
                src_ref=src.at[d],
                dst_ref=dst.at[me],
                send_sem=ss,
                recv_sem=rs,
                device_id=device(d),
                device_id_type=MESH,
            ).start()
            return 0

        lax.fori_loop(1, SLOTS, go, 0)
        own = pltpu.make_async_copy(src.at[me], dst.at[me], own_at)
        own.start()
        return own

    def finish(own, src, dst, ss, rs):
        own.wait()
        rest = pl.ds(0, SLOTS - 1)
        pltpu.make_async_remote_copy(
            src_ref=src.at[rest],
            dst_ref=dst.at[rest],
            send_sem=ss,
            recv_sem=rs,
            device_id=(row, col),
            device_id_type=MESH,
        ).wait()

    own = exchange(send1, recv1, ss_1, rs_1, own_sem.at[1])
    green_into(green_ref, h_ref, first)
    finish(own, send1, recv1, ss_1, rs_1)
    forward_into(recv1, ey, ez, lhs_f, s_ref, first)
    owns = []
    for a in range(3):
        back_into(a, h_ref, s_ref, q_ref, zt, ey, send2, first)
        owns.append(exchange(send2.at[a], recv2.at[a], ss_2.at[a], rs_2.at[a], own_sem.at[2 + a]))
    for a in range(3):
        finish(owns[a], send2.at[a], recv2.at[a], ss_2.at[a], rs_2.at[a])
        parts = [jnp.concatenate([recv2[a, :, 2 * part, :], recv2[a, :, 2 * part + 1, :]], axis=1) for part in range(2)]
        field = dot3((xi[0][...], xi[1][...]), split(jnp.concatenate(parts, axis=0)))
        hi, lo = split(field[:, :ROWS])
        table_ref[128 * a : 128 * a + 128] = jnp.concatenate([hi, lo, hi], axis=1)


def field_of(operands, blk=2048, n=512):
    ops = [o.reshape(1, -1) if o.ndim == 1 else o for o in operands]
    assert len(ops) == N_IN
    cap = 128
    dma = pltpu.SemaphoreType.DMA
    return pl.pallas_call(
        functools.partial(field_kernel, n=n),
        name="field",
        out_shape=(jax.ShapeDtypeStruct((384, 3 * ROWS), BF), jax.ShapeDtypeStruct((9, N_COL * cap), F32)),
        in_specs=[pl.BlockSpec(memory_space=pltpu.MemorySpace.HBM)] * N_IN,
        out_specs=(pl.BlockSpec(memory_space=pltpu.VMEM),) * 2,
        scratch_shapes=[pltpu.VMEM(o.shape, o.dtype) for o in ops]
        + [
            pltpu.VMEM((3 * 512, ops[0].shape[1]), BF),
            pltpu.VMEM((N_COL, 9, cap), F32),
            pltpu.VMEM((N_COL, 9, cap), F32),
            pltpu.VMEM((2 * ROWS, blk), BF),
            pltpu.VMEM((256, blk), BF),
            pltpu.VMEM((2 * ROWS, 256), F32),
            pltpu.VMEM((SLOTS, 4, 128), F32),
            pltpu.VMEM((SLOTS, 4, 128), F32),
            pltpu.VMEM((3, 4, 256, 256), F32),
            pltpu.VMEM((2, 384, 1024), BF),
            pltpu.VMEM((4, 256, 256), F32),
            pltpu.VMEM((2, 256, 256), F32),
            pltpu.VMEM((3, SLOTS, 4, 128), F32),
            pltpu.VMEM((3, SLOTS, 4, 128), F32),
            dma((N_IN,)),
            dma((5,)),
            dma(()),
            dma(()),
            dma(()),
            dma(()),
            dma((3,)),
            dma((3,)),
        ],
        compiler_params=pltpu.CompilerParams(vmem_limit_bytes=56 << 20, has_side_effects=True, collective_id=0),
    )(*ops)


def body(
    resident_cell,
    resident_corner,
    resident_frac,
    resident_charge,
    resident_momentum,
    migrant_dest,
    migrant_cell,
    migrant_corner,
    migrant_frac,
    migrant_charge,
    migrant_momentum,
    green,
):
    consts = [jnp.asarray(t) for pair in tables() for t in pair]
    stayed = (resident_cell, resident_corner, resident_frac, resident_charge)
    field, moved = field_of(
        [
            migrant_dest.reshape(-1),
            migrant_cell,
            migrant_corner,
            migrant_frac,
            migrant_charge,
            migrant_momentum,
            *stayed,
            green,
            *consts,
        ]
    )
    went = (moved[7].astype(I32), moved[8].astype(I32), moved[0:3], moved[3])
    return kick(field, *stayed, resident_momentum), kick(field, *went, moved[4:7])


def solution(mesh):
    both = ("row", "col")
    in_specs = (
        P(both),
        P(both),
        P(None, both),
        P(both),
        P(None, both),
        P(both, None),
        P(both),
        P(both),
        P(None, both),
        P(both),
        P(None, both),
        P(None, None, both, None, None),
    )
    out_specs = (P(None, both), P(None, both))
    return jax.shard_map(body, mesh=mesh, in_specs=in_specs, out_specs=out_specs, check_vma=False)
```

```python
import functools

import jax
import jax.numpy as jnp
import numpy as np
from jax import lax
from jax.experimental import pallas as pl
from jax.experimental.pallas import tpu as pltpu
from jax.sharding import PartitionSpec as P

F32, BF, I32, F8 = jnp.float32, jnp.bfloat16, jnp.int32, jnp.float8_e4m3fn
N_ROW, N_COL = 4, 32
SLOTS = N_ROW * N_COL
ROWS = 208
PAD = 256
BIG = 60 << 20


def split_np(table):
    hi = table.astype(jnp.bfloat16)
    return hi, (table - hi.astype(np.float64)).astype(jnp.bfloat16)


def row_places():
    layer, y = np.full(PAD, -1), np.zeros(PAD, int)
    layer[:192], y[:192] = np.arange(192) // 32, np.arange(192) % 32
    for side in range(2):
        layer[192 + 8 * side : 198 + 8 * side] = np.arange(6)
        y[192 + 8 * side : 200 + 8 * side] = 33 * side - 1
    return layer, y


def tables():
    wave = np.arange(256)
    layer, y = row_places()
    yg = 32 * np.arange(N_ROW)[:, None] + y[None]
    live = ((layer >= 0)[None] & (yg >= 0) & (yg < 128)).reshape(-1, 1)
    angle = 2 * np.pi / 256 * (yg.reshape(-1, 1) * wave % 256)
    ey = np.concatenate([np.cos(angle), np.sin(angle)], axis=1) * live
    zg = (4 * np.arange(N_COL)[None] + np.arange(6)[:, None] - 1).reshape(-1)
    live = ((zg >= 0) & (zg < 128))[None]
    angle = 2 * np.pi / 256 * (wave[:, None] * zg % 256)
    ez = np.stack([np.cos(angle) * live, np.sin(angle) * live])
    ezt = ez.transpose(0, 2, 1).reshape(384, 256)
    x, j = np.arange(128), np.arange(128)
    angle = 2 * np.pi / 256 * (j[:, None] * x % 256)
    imag = -np.sin(angle)
    imag[0] = 1 - 2 * (x % 2)
    dx = np.concatenate([np.cos(angle), imag])
    return [split_np(t) for t in (ey, ez.reshape(512, 192), ezt, dx, dx.T / 256.0**3)]


def split(v):
    hi = v.astype(BF)
    return hi, (v - hi.astype(F32)).astype(BF)


def dot3(a, b, dims=((1,), (0,))):
    one = lambda p, q: lax.dot_general(p, q, (dims, ((), ())), preferred_element_type=F32)
    return one(a[0], b[0]) + (one(a[0], b[1]) + one(a[1], b[0]))


def tile16(row, n):
    return jnp.broadcast_to(row, (16, n)).astype(BF)


def yz_weights(cell, corner, fy, fz, q, n, write):
    y = (cell >> 7) & 31
    z = (cell >> 12) + 1
    yfar = y + ((corner >> 1) & 1) * 2 - 1
    zfar = z + ((corner >> 2) & 1) * 2 - 1
    io8 = lax.broadcasted_iota(I32, (8, n), 0)
    wz = jnp.where(io8 == z, (1.0 - fz) * q, jnp.where(io8 == zfar, fz * q, 0.0))
    near = wz * (1.0 - fy)
    far = wz * fy
    nh = near.astype(BF).astype(F32); nl = near - nh
    fh = far.astype(BF).astype(F32); fl = far - fh
    io16 = lax.broadcasted_iota(I32, (16, n), 0).astype(BF)
    yb = jnp.broadcast_to(y.astype(F32), (16, n)).astype(BF)
    yfb = jnp.broadcast_to(yfar.astype(F32), (16, n)).astype(BF)
    zero = jnp.zeros((16, n), BF)
    masks = [(yb == io16, yfb == io16), (yb == io16 + 16.0, yfb == io16 + 16.0)]
    for ze in range(6):
        a, b, c, d = (tile16(v[ze:ze+1], n) for v in (nh, fh, nl, fl))
        for h in range(2):
            mn, mf = masks[h]
            write(ze*32 + h*16, jnp.where(mn, a, jnp.where(mf, b, zero)), jnp.where(mn, c, jnp.where(mf, d, zero)))
    isb = yfar < 0
    isa = yfar > 31
    rh = jnp.concatenate([jnp.where(isb, fh, 0.0), jnp.where(isa, fh, 0.0)], axis=0).astype(BF)
    rl = jnp.concatenate([jnp.where(isb, fl, 0.0), jnp.where(isa, fl, 0.0)], axis=0).astype(BF)
    write(192, rh, rl)

def x_weights(cell, corner, fx, n, write):
    x = cell & 127
    xfar = x + (corner & 1) * 2 - 1
    gx = 1.0 - fx
    gh = gx.astype(BF).astype(F32)
    fh = fx.astype(BF).astype(F32)
    gh, gl, fh, fl = (tile16(v, n) for v in (gh, gx - gh, fh, fx - fh))
    io16 = lax.broadcasted_iota(I32, (16, n), 0).astype(BF)
    xb, xfb = tile16(x.astype(F32), n), tile16(xfar.astype(F32), n)
    zero = jnp.zeros((16, n), BF)
    for t in range(8):
        near, far = xb == io16 + BF(16 * t), xfb == io16 + BF(16 * t)
        write(16 * t, jnp.where(near, gh, jnp.where(far, fh, zero)), jnp.where(near, gl, jnp.where(far, fl, zero)))


def deposit_block(rows, a_ref, b_ref, acc_ref, n):
    for s in range(a_ref.shape[1] // n):
        here = pl.ds(s * n, n)
        cell, corner, fx, fy, fz, q = rows(s)

        def write_a(r, hi, lo):
            a_ref[r : r + 16, here] = hi
            a_ref[ROWS + r : ROWS + r + 16, here] = lo

        def write_b(r, hi, lo):
            b_ref[r : r + 16, here] = hi
            b_ref[128 + r : 128 + r + 16, here] = lo

        yz_weights(cell, corner, fy, fz, q, n, write_a)
        x_weights(cell, corner, fx, n, write_b)
    acc_ref[...] += lax.dot_general(a_ref[...], b_ref[...], (((1,), (1,)), ((), ())), preferred_element_type=F32)


def pack_into(dest_ref, cell_ref, corner_ref, frac_ref, q_ref, mom_ref, lhs_ref, out_ref):
    total = dest_ref.shape[-1]
    dest = dest_ref[...]
    hits = (lax.broadcasted_iota(I32, (N_COL, total), 0) == dest).astype(F32)
    upper = (lax.broadcasted_iota(I32, (256, 256), 0) < lax.broadcasted_iota(I32, (256, 256), 1)).astype(BF)
    carry = jnp.zeros((N_COL, 1), F32)
    ranks = []
    for s in range(0, total, 256):
        part = hits[:, s : s + 256]
        before = jnp.dot(part.astype(BF), upper, preferred_element_type=F32) + carry
        carry = carry + jnp.sum(part, axis=1, keepdims=True)
        ranks.append(jnp.sum(part * before, axis=0, keepdims=True))
    rank = jnp.concatenate(ranks, axis=1)
    cap = out_ref.shape[-1]
    choose = (lax.broadcasted_iota(I32, (cap, total), 0).astype(F32) == rank).astype(BF)
    payload = jnp.concatenate(
        [
            frac_ref[...],
            q_ref[...],
            mom_ref[...],
            cell_ref[...].astype(F32),
            corner_ref[...].astype(F32),
            jnp.zeros((7, total), F32),
        ],
        axis=0,
    )
    hi = payload.astype(BF)
    rest = payload - hi.astype(F32)
    mid = rest.astype(BF)
    low = (rest - mid.astype(F32)).astype(BF)
    destb = tile16(dest.astype(F32), total)
    zero = jnp.zeros((16, total), BF)
    for d in range(N_COL):
        mask = destb == BF(d)
        for i, piece in enumerate((hi, mid, low)):
            lhs_ref[i * 512 + d * 16 : i * 512 + d * 16 + 16] = jnp.where(mask, piece, zero)
    got = lax.dot_general(lhs_ref[...], choose, (((1,), (1,)), ((), ())), preferred_element_type=F32)
    got = (got[:512] + got[512:1024]) + got[1024:]
    for d in range(N_COL):
        out_ref[d] = got[d * 16 : d * 16 + 9]


def yz_tiles(cell, corner, fy, fz, q, n, write):
    y = (cell >> 7) & 31
    z = (cell >> 12) + 1
    yfar = y + ((corner >> 1) & 1) * 2 - 1
    zfar = z + ((corner >> 2) & 1) * 2 - 1
    io8 = lax.broadcasted_iota(I32, (8, n), 0)
    wz = jnp.where(io8 == z, (1.0 - fz) * q, jnp.where(io8 == zfar, fz * q, 0.0))
    near = wz * (1.0 - fy)
    far = wz * fy
    nh = near.astype(BF).astype(F32)
    fh = far.astype(BF).astype(F32)
    nl, fl = (near - nh) * 4096.0, (far - fh) * 4096.0

    def big(row):
        half = tile16(row, n)
        return jnp.concatenate([half, half], axis=0)

    io = lax.broadcasted_iota(I32, (32, n), 0).astype(F32).astype(BF)
    at_near, at_far = big(y.astype(F32)) == io, big(yfar.astype(F32)) == io
    zero = jnp.zeros((32, n), BF)
    for ze in range(6):
        a, b, c, d = (big(v[ze : ze + 1]) for v in (nh, fh, nl, fl))
        write(ze * 32, jnp.where(at_near, a, jnp.where(at_far, b, zero)), jnp.where(at_near, c, jnp.where(at_far, d, zero)))
    below, above = yfar < 0, yfar > 31
    rims = [
        jnp.concatenate([jnp.where(below, v, 0.0), jnp.where(above, v, 0.0), jnp.zeros((16, n), F32)], axis=0)
        for v in (fh, fl)
    ]
    write(192, rims[0].astype(BF), rims[1].astype(BF))


def kick_chunk(ft_ref, f8_ref, w_ref, w8_ref, here, n, rows):
    cell, corner, fx, fy, fz, q = rows

    def write(r, hi, lo):
        w_ref[r : r + 32, here] = hi
        w8_ref[r : r + 32, here] = hi.astype(F8)
        w8_ref[PAD + r : PAD + r + 32, here] = lo.astype(F8)

    yz_tiles(cell, corner, fy, fz, q, n, write)
    got = jnp.dot(ft_ref[...], w_ref[:, here], preferred_element_type=F32)
    more = jnp.dot(f8_ref[...], w8_ref[:, here], preferred_element_type=F32)
    x = cell & 127
    xfar = x + (corner & 1) * 2 - 1
    io = lax.broadcasted_iota(I32, (128, n), 0)
    wx = jnp.where(io == x, 1.0 - fx, jnp.where(io == xfar, fx, 0.0))
    total = got + more
    return [jnp.sum(total[a * 128 : a * 128 + 128] * wx, axis=0, keepdims=True) for a in range(3)]


def kick_kernel(*refs, n):
    hbm, (out_hbm, migrant_ref), held = refs[:9], refs[9:11], refs[11:20]
    out_ref, w_ref, w8_ref, made_sem, in_sem, out_sem = refs[20:]
    made = [pltpu.make_async_copy(hbm[i], held[i], made_sem.at[i]) for i in range(4)]
    for copy in made:
        copy.start()
    (ft_ref, f8_ref, scale_ref, moved_ref), hbm, held = held[:4], hbm[4:], held[4:]
    cell_ref, corner_ref, frac_ref, q_ref, mom_ref = held
    blk = w_ref.shape[1]
    total = cell_ref.shape[1]
    pieces = (pl.ds(0, blk), pl.ds(blk, total - blk))
    copies = [
        [pltpu.make_async_copy(h.at[:, p], v.at[:, p], in_sem.at[j, i]) for i, (h, v) in enumerate(zip(hbm, held))]
        for j, p in enumerate(pieces)
    ]
    for copy in copies[0] + copies[1]:
        copy.start()
    for r in (224, 480):
        w8_ref[r : r + 32] = jnp.zeros((32, blk), F8)
    w_ref[224:] = jnp.zeros((32, blk), BF)
    chunk = functools.partial(kick_chunk, ft_ref, f8_ref, w_ref, w8_ref)
    for copy in made:
        copy.wait()

    def migrants(i, _):
        for s in range(blk // n):
            here = pl.ds(pl.multiple_of(i * blk + s * n, n), n)
            got = moved_ref[:, here]
            rows = (got[7:8].astype(I32), got[8:9].astype(I32), got[0:1], got[1:2], got[2:3], got[3:4])
            kicks = chunk(pl.ds(s * n, n), n, rows)
            for a in range(3):
                migrant_ref[a : a + 1, here] = got[4 + a : 5 + a] + kicks[a] * scale_ref[a : a + 1, 0:1]
        return 0

    lax.fori_loop(0, moved_ref.shape[1] // blk, migrants, 0)
    for copy in copies[0]:
        copy.wait()

    def residents(i, _):
        @pl.when(i == 1)
        def _():
            for copy in copies[1]:
                copy.wait()

        for s in range(blk // n):
            here = pl.ds(pl.multiple_of(i * blk + s * n, n), n)
            rows = (
                cell_ref[:, here],
                corner_ref[:, here],
                frac_ref[0:1, here],
                frac_ref[1:2, here],
                frac_ref[2:3, here],
                q_ref[:, here],
            )
            kicks = chunk(pl.ds(s * n, n), n, rows)
            for a in range(3):
                out_ref[a : a + 1, here] = mom_ref[a : a + 1, here] + kicks[a] * scale_ref[a : a + 1, 0:1]
        block = pl.ds(pl.multiple_of(i * blk, blk), blk)
        pltpu.make_async_copy(out_ref.at[:, block], out_hbm.at[:, block], out_sem).start()
        return 0

    lax.fori_loop(0, total // blk, residents, 0)
    pltpu.make_async_copy(out_ref, out_hbm, out_sem).wait()


def kick(tables_of, moved, cell, corner, frac, q, mom, blk=4096, n=256):
    ops = [*tables_of, moved, cell.reshape(1, -1), corner.reshape(1, -1), frac, q.reshape(1, -1), mom]
    vmem, hbm = (pl.BlockSpec(memory_space=s) for s in (pltpu.VMEM, pltpu.MemorySpace.HBM))
    return pl.pallas_call(
        functools.partial(kick_kernel, n=n),
        name="kick",
        out_shape=(jax.ShapeDtypeStruct(mom.shape, F32), jax.ShapeDtypeStruct((3, moved.shape[1]), F32)),
        in_specs=[hbm] * 9,
        out_specs=(hbm, vmem),
        scratch_shapes=[pltpu.VMEM(o.shape, o.dtype) for o in ops]
        + [
            pltpu.VMEM(mom.shape, F32),
            pltpu.VMEM((PAD, blk), BF),
            pltpu.VMEM((2 * PAD, blk), F8),
            pltpu.SemaphoreType.DMA((4,)),
            pltpu.SemaphoreType.DMA((2, 5)),
            pltpu.SemaphoreType.DMA(()),
        ],
        compiler_params=pltpu.CompilerParams(vmem_limit_bytes=BIG),
    )(*ops)


def layer_of(shape):
    lane = lax.broadcasted_iota(I32, shape, 1)
    return jnp.where(lane < 192, lane // 32, jnp.where(lane < ROWS, lane % 8, 6))


def green_into(green_ref, h_ref, first):
    index = lax.broadcasted_iota(I32, (256, 256), 0) + lax.broadcasted_iota(I32, (256, 256), 1)
    mirror = ((index == 0) | (index == 256)).astype(BF)

    def flip(plane):
        half = jnp.dot(mirror, plane, preferred_element_type=F32).astype(BF)
        return jnp.dot(half, mirror, preferred_element_type=F32)

    @pl.when(first)
    def _():
        for a in range(3):
            for sign in range(2):
                real, imag = green_ref[a, 0, sign], green_ref[a, 1, sign]
                h_ref[a, 2 * sign] = 0.5 * (real.astype(F32) + flip(real))
                h_ref[a, 2 * sign + 1] = 0.5 * (imag.astype(F32) - flip(imag))

    @pl.when(jnp.logical_not(first))
    def _():
        for a in range(3):
            h_ref[a, 0] = green_ref[a, 0, 0].astype(F32) + flip(green_ref[a, 0, 1])
            h_ref[a, 1] = green_ref[a, 1, 0].astype(F32) - flip(green_ref[a, 1, 1])


def forward_into(got_ref, ey, ez, lhs_ref, s_ref, first):
    layer = layer_of((N_COL, PAD))
    for part in range(2):
        for r in range(N_ROW):
            rows = slice(32 * r, 32 * r + 32)
            both = jnp.concatenate([got_ref[rows, 2 * part, :], got_ref[rows, 2 * part + 1, :]], axis=1)
            for ze in range(6):
                hi, lo = split(jnp.where(layer == ze, both, 0.0))
                where = slice(192 * part + 32 * ze, 192 * part + 32 * ze + 32)
                lhs_ref[0, where, PAD * r : PAD * r + PAD] = hi
                lhs_ref[1, where, PAD * r : PAD * r + PAD] = lo
    u = dot3((lhs_ref[0], lhs_ref[1]), (ey[0][...], ey[1][...]))
    re_c, re_s, im_c, im_s = u[:192, :256], u[:192, 256:], u[192:, :256], u[192:, 256:]
    ezs = (ez[0][...], ez[1][...])

    def forward(real, imag):
        v = dot3(ezs, split(jnp.concatenate([real, imag], axis=1)))
        return v[:256, :256] + v[256:, 256:], v[:256, 256:] - v[256:, :256]

    @pl.when(first)
    def _():
        s_ref[0], s_ref[1] = forward(re_c, -re_s)
        s_ref[2], s_ref[3] = forward(im_c, -im_s)

    @pl.when(jnp.logical_not(first))
    def _():
        s_ref[0], s_ref[1] = forward(re_c + im_s, im_c - re_s)


def back_into(a, h_ref, s_ref, q_ref, zt, ey, out_ref, first):
    layer = layer_of((N_COL, PAD))
    a_re = s_ref[0] * h_ref[a, 0] - s_ref[1] * h_ref[a, 1]
    a_im = s_ref[0] * h_ref[a, 1] + s_ref[1] * h_ref[a, 0]
    q_ref[0], q_ref[1] = a_re, a_im

    @pl.when(first)
    def _():
        b_re = s_ref[2] * h_ref[a, 2] - s_ref[3] * h_ref[a, 3]
        b_im = s_ref[2] * h_ref[a, 3] + s_ref[3] * h_ref[a, 2]
        q_ref[0] = q_ref[0] - b_im
        q_ref[1] = q_ref[1] + b_re

    q = split(jnp.concatenate([q_ref[0], q_ref[1]], axis=1))
    v = dot3((zt[0][...], zt[1][...]), q)
    v = jnp.concatenate([v[:192, :256] - v[192:, 256:], v[:192, 256:] + v[192:, :256]], axis=0)
    v = split(v)
    for r in range(N_ROW):
        rows = slice(PAD * r, PAD * r + PAD)
        cos = dot3(v, (ey[0][rows, :256], ey[1][rows, :256]), ((1,), (1,)))
        sin = dot3(v, (ey[0][rows, 256:], ey[1][rows, 256:]), ((1,), (1,)))
        w = (cos[:192] - sin[192:], cos[192:] + sin[:192])
        for part in range(2):
            mine = jnp.zeros((N_COL, PAD), F32)
            for ze in range(6):
                mine = jnp.where(layer == ze, w[part][32 * ze : 32 * ze + 32], mine)
            for half in range(2):
                out_ref[a, 32 * r : 32 * r + 32, 2 * part + half, :] = mine[:, 128 * half : 128 * half + 128]


MESH = pl.DeviceIdType.MESH
N_IN = 21


def field_kernel(*refs, n):
    hbm, (ft_ref, f8_ref, scale_ref, moved_ref) = refs[:N_IN], refs[N_IN : N_IN + 4]
    held = refs[N_IN + 4 : 2 * N_IN + 4]
    (lhs_p, pack_s, pack_r, a_ref, b_ref, acc_ref, send1, recv1, h_ref, lhs_f, s_ref, q_ref, send2, recv2) = refs[
        2 * N_IN + 4 : 2 * N_IN + 18
    ]
    in_sem, own_sem, ss_m, rs_m, ss_1, rs_1, ss_2, rs_2 = refs[2 * N_IN + 18 :]
    row, col = lax.axis_index("row"), lax.axis_index("col")
    me = row * N_COL + col
    first = me == 0

    def device(d):
        return (d >> 5, d & 31)

    copies = [pltpu.make_async_copy(h, v, in_sem.at[i]) for i, (h, v) in enumerate(zip(hbm, held))]
    for copy in copies:
        copy.start()

    barrier = pltpu.get_barrier_semaphore()

    def greet(i, _):
        pl.semaphore_signal(barrier, inc=1, device_id=device((me + i) & 127), device_id_type=MESH)
        return 0

    lax.fori_loop(1, SLOTS, greet, 0)
    acc_ref[...] = jnp.zeros_like(acc_ref)

    for copy in copies[:6]:
        copy.wait()
    pack_into(*held[:6], lhs_p, pack_s)
    for copy in copies[6:10]:
        copy.wait()
    cell_ref, corner_ref, frac_ref, q_in = held[6:10]
    blk = a_ref.shape[1]
    steps = cell_ref.shape[1] // blk

    def resident(i, _):
        def rows(s):
            here = pl.ds(pl.multiple_of(i * blk + s * n, n), n)
            return (
                cell_ref[:, here],
                corner_ref[:, here],
                frac_ref[0:1, here],
                frac_ref[1:2, here],
                frac_ref[2:3, here],
                q_in[:, here],
            )

        deposit_block(rows, a_ref, b_ref, acc_ref, n)
        return 0

    lax.fori_loop(0, steps // 2, resident, 0)
    pl.semaphore_wait(barrier, SLOTS - 1)

    def send_migrants(i, _):
        c = (col + i) & 31
        pltpu.make_async_remote_copy(
            src_ref=pack_s.at[c],
            dst_ref=pack_r.at[col],
            send_sem=ss_m,
            recv_sem=rs_m,
            device_id=(row, c),
            device_id_type=MESH,
        ).start()
        return 0

    lax.fori_loop(1, N_COL, send_migrants, 0)
    own = pltpu.make_async_copy(pack_s.at[col], pack_r.at[col], own_sem.at[0])
    own.start()
    lax.fori_loop(steps // 2, steps, resident, 0)
    own.wait()
    rest = pl.ds(0, N_COL - 1)
    pltpu.make_async_remote_copy(
        src_ref=pack_s.at[rest],
        dst_ref=pack_r.at[rest],
        send_sem=ss_m,
        recv_sem=rs_m,
        device_id=(row, col),
        device_id_type=MESH,
    ).wait()
    for s in range(N_COL):
        moved_ref[:, 128 * s : 128 * s + 128] = pack_r[s]

    def migrant(i, _):
        def rows(s):
            here = pl.ds(pl.multiple_of(i * blk + s * n, n), n)
            got = moved_ref[:, here]
            return (
                got[7:8].astype(I32),
                got[8:9].astype(I32),
                got[0:1],
                got[1:2],
                got[2:3],
                got[3:4],
            )

        deposit_block(rows, a_ref, b_ref, acc_ref, n)
        return 0

    lax.fori_loop(0, moved_ref.shape[1] // blk, migrant, 0)
    for copy in copies[10:]:
        copy.wait()
    green_ref = held[10]
    ey, ez, zt, dx, xi = (held[11 + 2 * i : 13 + 2 * i] for i in range(5))

    acc = acc_ref[...]
    grid = (acc[:ROWS, :128] + acc[ROWS:, 128:]) + (acc[:ROWS, 128:] + acc[ROWS:, :128])
    sent = dot3((dx[0][...], dx[1][...]), split(grid), ((1,), (1,)))
    sent = jnp.concatenate([sent, jnp.zeros((256, PAD - ROWS), F32)], axis=1)
    for part in range(2):
        for half in range(2):
            send1[:, 2 * part + half, :] = sent[128 * part : 128 * part + 128, 128 * half : 128 * half + 128]

    def exchange(src, dst, ss, rs, own_at):
        def go(i, _):
            d = (me + i) & 127
            pltpu.make_async_remote_copy(
                src_ref=src.at[d],
                dst_ref=dst.at[me],
                send_sem=ss,
                recv_sem=rs,
                device_id=device(d),
                device_id_type=MESH,
            ).start()
            return 0

        lax.fori_loop(1, SLOTS, go, 0)
        own = pltpu.make_async_copy(src.at[me], dst.at[me], own_at)
        own.start()
        return own

    def finish(own, src, dst, ss, rs):
        own.wait()
        rest = pl.ds(0, SLOTS - 1)
        pltpu.make_async_remote_copy(
            src_ref=src.at[rest],
            dst_ref=dst.at[rest],
            send_sem=ss,
            recv_sem=rs,
            device_id=(row, col),
            device_id_type=MESH,
        ).wait()

    own = exchange(send1, recv1, ss_1, rs_1, own_sem.at[1])
    green_into(green_ref, h_ref, first)
    finish(own, send1, recv1, ss_1, rs_1)
    forward_into(recv1, ey, ez, lhs_f, s_ref, first)
    owns = []
    for a in range(3):
        back_into(a, h_ref, s_ref, q_ref, zt, ey, send2, first)
        owns.append(exchange(send2.at[a], recv2.at[a], ss_2.at[a], rs_2.at[a], own_sem.at[2 + a]))
    for a in range(3):
        finish(owns[a], send2.at[a], recv2.at[a], ss_2.at[a], rs_2.at[a])
        parts = [jnp.concatenate([recv2[a, :, 2 * part, :], recv2[a, :, 2 * part + 1, :]], axis=1) for part in range(2)]
        field = dot3((xi[0][...], xi[1][...]), split(jnp.concatenate(parts, axis=0)))
        top = jnp.max(jnp.max(jnp.abs(field), axis=0, keepdims=True), axis=1, keepdims=True)
        top = jnp.maximum(top, 1e-30)
        field = field / top
        hi = field.astype(BF).astype(F32)
        here = slice(128 * a, 128 * a + 128)
        ft_ref[here] = (hi * 65536.0).astype(BF)
        f8_ref[here, :PAD] = ((field - hi) * 65536.0).astype(F8)
        f8_ref[here, PAD:] = (hi * 16.0).astype(F8)
        scale_ref[a : a + 1] = jnp.broadcast_to(top * (1.0 / 65536.0), (1, 128))
    scale_ref[3:] = jnp.zeros((5, 128), F32)


def field_of(operands, blk=2048, n=512):
    ops = [o.reshape(1, -1) if o.ndim == 1 else o for o in operands]
    assert len(ops) == N_IN
    cap = 128
    dma = pltpu.SemaphoreType.DMA
    return pl.pallas_call(
        functools.partial(field_kernel, n=n),
        name="field",
        out_shape=(
            jax.ShapeDtypeStruct((384, PAD), BF),
            jax.ShapeDtypeStruct((384, 2 * PAD), F8),
            jax.ShapeDtypeStruct((8, 128), F32),
            jax.ShapeDtypeStruct((9, N_COL * cap), F32),
        ),
        in_specs=[pl.BlockSpec(memory_space=pltpu.MemorySpace.HBM)] * N_IN,
        out_specs=(pl.BlockSpec(memory_space=pltpu.VMEM),) * 4,
        scratch_shapes=[pltpu.VMEM(o.shape, o.dtype) for o in ops]
        + [
            pltpu.VMEM((3 * 512, ops[0].shape[1]), BF),
            pltpu.VMEM((N_COL, 9, cap), F32),
            pltpu.VMEM((N_COL, 9, cap), F32),
            pltpu.VMEM((2 * ROWS, blk), BF),
            pltpu.VMEM((256, blk), BF),
            pltpu.VMEM((2 * ROWS, 256), F32),
            pltpu.VMEM((SLOTS, 4, 128), F32),
            pltpu.VMEM((SLOTS, 4, 128), F32),
            pltpu.VMEM((3, 4, 256, 256), F32),
            pltpu.VMEM((2, 384, 1024), BF),
            pltpu.VMEM((4, 256, 256), F32),
            pltpu.VMEM((2, 256, 256), F32),
            pltpu.VMEM((3, SLOTS, 4, 128), F32),
            pltpu.VMEM((3, SLOTS, 4, 128), F32),
            dma((N_IN,)),
            dma((5,)),
            dma(()),
            dma(()),
            dma(()),
            dma(()),
            dma((3,)),
            dma((3,)),
        ],
        compiler_params=pltpu.CompilerParams(vmem_limit_bytes=BIG, has_side_effects=True, collective_id=0),
    )(*ops)


def body(
    resident_cell,
    resident_corner,
    resident_frac,
    resident_charge,
    resident_momentum,
    migrant_dest,
    migrant_cell,
    migrant_corner,
    migrant_frac,
    migrant_charge,
    migrant_momentum,
    green,
):
    consts = [jnp.asarray(t) for pair in tables() for t in pair]
    stayed = (resident_cell, resident_corner, resident_frac, resident_charge)
    *field, moved = field_of(
        [
            migrant_dest.reshape(-1),
            migrant_cell,
            migrant_corner,
            migrant_frac,
            migrant_charge,
            migrant_momentum,
            *stayed,
            green,
            *consts,
        ]
    )
    return kick(field, moved, *stayed, resident_momentum)


def solution(mesh):
    both = ("row", "col")
    in_specs = (
        P(both),
        P(both),
        P(None, both),
        P(both),
        P(None, both),
        P(both, None),
        P(both),
        P(both),
        P(None, both),
        P(both),
        P(None, both),
        P(None, None, both, None, None),
    )
    out_specs = (P(None, both), P(None, both))
    return jax.shard_map(body, mesh=mesh, in_specs=in_specs, out_specs=out_specs, check_vma=False)
```

```python
import functools

import jax
import jax.numpy as jnp
import numpy as np
from jax import lax
from jax.experimental import pallas as pl
from jax.experimental.pallas import tpu as pltpu
from jax.sharding import PartitionSpec as P

F32, BF, I32, F8 = jnp.float32, jnp.bfloat16, jnp.int32, jnp.float8_e4m3fn
N_ROW, N_COL = 4, 32
SLOTS = N_ROW * N_COL
ROWS = 208
PAD = 256
BIG = 60 << 20


def split_np(table):
    hi = table.astype(jnp.bfloat16)
    return hi, (table - hi.astype(np.float64)).astype(jnp.bfloat16)


def y_places():
    y = np.full(PAD, -1)
    y[:128] = np.arange(128)
    for r in range(N_ROW):
        for side in range(2):
            first = 128 + 16 * r + 8 * side
            y[first : first + 6] = 32 * r + 33 * side - 1
    return y


def tables():
    wave = np.arange(256)
    y = y_places()[:, None]
    angle = 2 * np.pi / 256 * (y * wave % 256)
    live = (y >= 0) & (y < 128)
    ey = np.concatenate([np.cos(angle), np.sin(angle)], axis=1) * live
    zg = (4 * np.arange(N_COL)[None] + np.arange(6)[:, None] - 1).reshape(-1)
    live = ((zg >= 0) & (zg < 128))[None]
    angle = 2 * np.pi / 256 * (wave[:, None] * zg % 256)
    ez = np.stack([np.cos(angle) * live, np.sin(angle) * live])
    ezt = ez.transpose(0, 2, 1).reshape(384, 256)
    x, j = np.arange(128), np.arange(128)
    angle = 2 * np.pi / 256 * (j[:, None] * x % 256)
    imag = -np.sin(angle)
    imag[0] = 1 - 2 * (x % 2)
    dx = np.concatenate([np.cos(angle), imag])
    return [split_np(t) for t in (ey, ez.reshape(512, 192), ezt, dx, dx.T / 256.0**3)]


def split(v):
    hi = v.astype(BF)
    return hi, (v - hi.astype(F32)).astype(BF)


def dot3(a, b, dims=((1,), (0,))):
    one = lambda p, q: lax.dot_general(p, q, (dims, ((), ())), preferred_element_type=F32)
    return one(a[0], b[0]) + (one(a[0], b[1]) + one(a[1], b[0]))


def tile16(row, n):
    return jnp.broadcast_to(row, (16, n)).astype(BF)


def yz_weights(cell, corner, fy, fz, q, n, write):
    y = (cell >> 7) & 31
    z = (cell >> 12) + 1
    yfar = y + ((corner >> 1) & 1) * 2 - 1
    zfar = z + ((corner >> 2) & 1) * 2 - 1
    io8 = lax.broadcasted_iota(I32, (8, n), 0)
    wz = jnp.where(io8 == z, (1.0 - fz) * q, jnp.where(io8 == zfar, fz * q, 0.0))
    near = wz * (1.0 - fy)
    far = wz * fy
    nh = near.astype(BF).astype(F32); nl = near - nh
    fh = far.astype(BF).astype(F32); fl = far - fh
    io16 = lax.broadcasted_iota(I32, (16, n), 0).astype(BF)
    yb = jnp.broadcast_to(y.astype(F32), (16, n)).astype(BF)
    yfb = jnp.broadcast_to(yfar.astype(F32), (16, n)).astype(BF)
    zero = jnp.zeros((16, n), BF)
    masks = [(yb == io16, yfb == io16), (yb == io16 + 16.0, yfb == io16 + 16.0)]
    for ze in range(6):
        a, b, c, d = (tile16(v[ze:ze+1], n) for v in (nh, fh, nl, fl))
        for h in range(2):
            mn, mf = masks[h]
            write(ze*32 + h*16, jnp.where(mn, a, jnp.where(mf, b, zero)), jnp.where(mn, c, jnp.where(mf, d, zero)))
    isb = yfar < 0
    isa = yfar > 31
    rh = jnp.concatenate([jnp.where(isb, fh, 0.0), jnp.where(isa, fh, 0.0)], axis=0).astype(BF)
    rl = jnp.concatenate([jnp.where(isb, fl, 0.0), jnp.where(isa, fl, 0.0)], axis=0).astype(BF)
    write(192, rh, rl)

def x_weights(cell, corner, fx, n, write):
    x = cell & 127
    xfar = x + (corner & 1) * 2 - 1
    gx = 1.0 - fx
    gh = gx.astype(BF).astype(F32)
    fh = fx.astype(BF).astype(F32)
    gh, gl, fh, fl = (tile16(v, n) for v in (gh, gx - gh, fh, fx - fh))
    io16 = lax.broadcasted_iota(I32, (16, n), 0).astype(BF)
    xb, xfb = tile16(x.astype(F32), n), tile16(xfar.astype(F32), n)
    zero = jnp.zeros((16, n), BF)
    for t in range(8):
        near, far = xb == io16 + BF(16 * t), xfb == io16 + BF(16 * t)
        write(16 * t, jnp.where(near, gh, jnp.where(far, fh, zero)), jnp.where(near, gl, jnp.where(far, fl, zero)))


def deposit_block(rows, a_ref, b_ref, acc_ref, n):
    for s in range(a_ref.shape[1] // n):
        here = pl.ds(s * n, n)
        cell, corner, fx, fy, fz, q = rows(s)

        def write_a(r, hi, lo):
            a_ref[r : r + 16, here] = hi
            a_ref[ROWS + r : ROWS + r + 16, here] = lo

        def write_b(r, hi, lo):
            b_ref[r : r + 16, here] = hi
            b_ref[128 + r : 128 + r + 16, here] = lo

        yz_weights(cell, corner, fy, fz, q, n, write_a)
        x_weights(cell, corner, fx, n, write_b)
    acc_ref[...] += lax.dot_general(a_ref[...], b_ref[...], (((1,), (1,)), ((), ())), preferred_element_type=F32)


def pack_into(dest_ref, cell_ref, corner_ref, frac_ref, q_ref, mom_ref, lhs_ref, out_ref):
    total = dest_ref.shape[-1]
    dest = dest_ref[...]
    hits = (lax.broadcasted_iota(I32, (N_COL, total), 0) == dest).astype(F32)
    upper = (lax.broadcasted_iota(I32, (256, 256), 0) < lax.broadcasted_iota(I32, (256, 256), 1)).astype(BF)
    carry = jnp.zeros((N_COL, 1), F32)
    ranks = []
    for s in range(0, total, 256):
        part = hits[:, s : s + 256]
        before = jnp.dot(part.astype(BF), upper, preferred_element_type=F32) + carry
        carry = carry + jnp.sum(part, axis=1, keepdims=True)
        ranks.append(jnp.sum(part * before, axis=0, keepdims=True))
    rank = jnp.concatenate(ranks, axis=1)
    cap = out_ref.shape[-1]
    choose = (lax.broadcasted_iota(I32, (cap, total), 0).astype(F32) == rank).astype(BF)
    payload = jnp.concatenate(
        [
            frac_ref[...],
            q_ref[...],
            mom_ref[...],
            cell_ref[...].astype(F32),
            corner_ref[...].astype(F32),
            jnp.zeros((7, total), F32),
        ],
        axis=0,
    )
    hi = payload.astype(BF)
    rest = payload - hi.astype(F32)
    mid = rest.astype(BF)
    low = (rest - mid.astype(F32)).astype(BF)
    destb = tile16(dest.astype(F32), total)
    zero = jnp.zeros((16, total), BF)
    for d in range(N_COL):
        mask = destb == BF(d)
        for i, piece in enumerate((hi, mid, low)):
            lhs_ref[i * 512 + d * 16 : i * 512 + d * 16 + 16] = jnp.where(mask, piece, zero)
    got = lax.dot_general(lhs_ref[...], choose, (((1,), (1,)), ((), ())), preferred_element_type=F32)
    got = (got[:512] + got[512:1024]) + got[1024:]
    for d in range(N_COL):
        out_ref[d] = got[d * 16 : d * 16 + 9]


def yz_tiles(cell, corner, fy, fz, q, n, write):
    y = (cell >> 7) & 31
    z = (cell >> 12) + 1
    yfar = y + ((corner >> 1) & 1) * 2 - 1
    zfar = z + ((corner >> 2) & 1) * 2 - 1
    io8 = lax.broadcasted_iota(I32, (8, n), 0)
    wz = jnp.where(io8 == z, (1.0 - fz) * q, jnp.where(io8 == zfar, fz * q, 0.0))
    near = wz * (1.0 - fy)
    far = wz * fy
    nh = near.astype(BF).astype(F32)
    fh = far.astype(BF).astype(F32)
    nl, fl = (near - nh) * 4096.0, (far - fh) * 4096.0

    def big(row):
        half = tile16(row, n)
        return jnp.concatenate([half, half], axis=0)

    io = lax.broadcasted_iota(I32, (32, n), 0).astype(F32).astype(BF)
    at_near, at_far = big(y.astype(F32)) == io, big(yfar.astype(F32)) == io
    zero = jnp.zeros((32, n), BF)
    for ze in range(6):
        a, b, c, d = (big(v[ze : ze + 1]) for v in (nh, fh, nl, fl))
        write(ze * 32, jnp.where(at_near, a, jnp.where(at_far, b, zero)), jnp.where(at_near, c, jnp.where(at_far, d, zero)))
    below, above = yfar < 0, yfar > 31
    rims = [
        jnp.concatenate([jnp.where(below, v, 0.0), jnp.where(above, v, 0.0), jnp.zeros((16, n), F32)], axis=0)
        for v in (fh, fl)
    ]
    write(192, rims[0].astype(BF), rims[1].astype(BF))


def kick_chunk(ft_ref, f8_ref, w_ref, w8_ref, here, n, rows):
    cell, corner, fx, fy, fz, q = rows

    def write(r, hi, lo):
        w_ref[r : r + 32, here] = hi
        w8_ref[r : r + 32, here] = hi.astype(F8)
        w8_ref[PAD + r : PAD + r + 32, here] = lo.astype(F8)

    yz_tiles(cell, corner, fy, fz, q, n, write)
    got = jnp.dot(ft_ref[...], w_ref[:, here], preferred_element_type=F32)
    more = jnp.dot(f8_ref[...], w8_ref[:, here], preferred_element_type=F32)
    x = cell & 127
    xfar = x + (corner & 1) * 2 - 1
    io = lax.broadcasted_iota(I32, (128, n), 0)
    wx = jnp.where(io == x, 1.0 - fx, jnp.where(io == xfar, fx, 0.0))
    total = got + more
    return [jnp.sum(total[a * 128 : a * 128 + 128] * wx, axis=0, keepdims=True) for a in range(3)]


def kick_kernel(*refs, n):
    hbm, (out_hbm, migrant_ref), held = refs[:9], refs[9:11], refs[11:20]
    out_ref, w_ref, w8_ref, made_sem, in_sem, out_sem = refs[20:]
    made = [pltpu.make_async_copy(hbm[i], held[i], made_sem.at[i]) for i in range(4)]
    for copy in made:
        copy.start()
    (ft_ref, f8_ref, scale_ref, moved_ref), hbm, held = held[:4], hbm[4:], held[4:]
    cell_ref, corner_ref, frac_ref, q_ref, mom_ref = held
    blk = w_ref.shape[1]
    total = cell_ref.shape[1]
    pieces = (pl.ds(0, blk), pl.ds(blk, total - blk))
    copies = [
        [pltpu.make_async_copy(h.at[:, p], v.at[:, p], in_sem.at[j, i]) for i, (h, v) in enumerate(zip(hbm, held))]
        for j, p in enumerate(pieces)
    ]
    for copy in copies[0] + copies[1]:
        copy.start()
    for r in (224, 480):
        w8_ref[r : r + 32] = jnp.zeros((32, blk), F8)
    w_ref[224:] = jnp.zeros((32, blk), BF)
    chunk = functools.partial(kick_chunk, ft_ref, f8_ref, w_ref, w8_ref)
    for copy in made:
        copy.wait()

    def migrants(i, _):
        for s in range(blk // n):
            here = pl.ds(pl.multiple_of(i * blk + s * n, n), n)
            got = moved_ref[:, here]
            rows = (got[7:8].astype(I32), got[8:9].astype(I32), got[0:1], got[1:2], got[2:3], got[3:4])
            kicks = chunk(pl.ds(s * n, n), n, rows)
            for a in range(3):
                migrant_ref[a : a + 1, here] = got[4 + a : 5 + a] + kicks[a] * scale_ref[a : a + 1, 0:1]
        return 0

    lax.fori_loop(0, moved_ref.shape[1] // blk, migrants, 0)
    for copy in copies[0]:
        copy.wait()

    def residents(i, _):
        @pl.when(i == 1)
        def _():
            for copy in copies[1]:
                copy.wait()

        for s in range(blk // n):
            here = pl.ds(pl.multiple_of(i * blk + s * n, n), n)
            rows = (
                cell_ref[:, here],
                corner_ref[:, here],
                frac_ref[0:1, here],
                frac_ref[1:2, here],
                frac_ref[2:3, here],
                q_ref[:, here],
            )
            kicks = chunk(pl.ds(s * n, n), n, rows)
            for a in range(3):
                out_ref[a : a + 1, here] = mom_ref[a : a + 1, here] + kicks[a] * scale_ref[a : a + 1, 0:1]
        block = pl.ds(pl.multiple_of(i * blk, blk), blk)
        pltpu.make_async_copy(out_ref.at[:, block], out_hbm.at[:, block], out_sem).start()
        return 0

    lax.fori_loop(0, total // blk, residents, 0)
    pltpu.make_async_copy(out_ref, out_hbm, out_sem).wait()


def kick(tables_of, moved, cell, corner, frac, q, mom, blk=4096, n=256):
    ops = [*tables_of, moved, cell.reshape(1, -1), corner.reshape(1, -1), frac, q.reshape(1, -1), mom]
    vmem, hbm = (pl.BlockSpec(memory_space=s) for s in (pltpu.VMEM, pltpu.MemorySpace.HBM))
    return pl.pallas_call(
        functools.partial(kick_kernel, n=n),
        name="kick",
        out_shape=(jax.ShapeDtypeStruct(mom.shape, F32), jax.ShapeDtypeStruct((3, moved.shape[1]), F32)),
        in_specs=[hbm] * 9,
        out_specs=(hbm, vmem),
        scratch_shapes=[pltpu.VMEM(o.shape, o.dtype) for o in ops]
        + [
            pltpu.VMEM(mom.shape, F32),
            pltpu.VMEM((PAD, blk), BF),
            pltpu.VMEM((2 * PAD, blk), F8),
            pltpu.SemaphoreType.DMA((4,)),
            pltpu.SemaphoreType.DMA((2, 5)),
            pltpu.SemaphoreType.DMA(()),
        ],
        compiler_params=pltpu.CompilerParams(vmem_limit_bytes=BIG),
    )(*ops)


def green_into(green_ref, h_ref, first):
    index = lax.broadcasted_iota(I32, (256, 256), 0) + lax.broadcasted_iota(I32, (256, 256), 1)
    mirror = ((index == 0) | (index == 256)).astype(BF)

    def flip(plane):
        half = jnp.dot(mirror, plane, preferred_element_type=F32).astype(BF)
        return jnp.dot(half, mirror, preferred_element_type=F32)

    @pl.when(first)
    def _():
        for a in range(3):
            for sign in range(2):
                real, imag = green_ref[a, 0, sign], green_ref[a, 1, sign]
                h_ref[a, 2 * sign] = 0.5 * (real.astype(F32) + flip(real))
                h_ref[a, 2 * sign + 1] = 0.5 * (imag.astype(F32) - flip(imag))

    @pl.when(jnp.logical_not(first))
    def _():
        for a in range(3):
            h_ref[a, 0] = green_ref[a, 0, 0].astype(F32) + flip(green_ref[a, 0, 1])
            h_ref[a, 1] = green_ref[a, 1, 0].astype(F32) - flip(green_ref[a, 1, 1])


def lanes(rows):
    return lax.broadcasted_iota(I32, (rows, 128), 1)


def turn(v, by):
    by = by % 128
    return pltpu.roll(v, by, 1) if by else v


def forward_into(got_ref, ey, ez, lhs_ref, s_ref, first):
    lane = lanes(N_COL)
    for part in range(2):
        inner = [jnp.zeros((N_COL, 128), F32)] * 6
        rims = jnp.zeros((N_COL, 128), F32)
        for r in range(N_ROW):
            rows = slice(32 * r, 32 * r + 32)
            low, high = got_ref[rows, 2 * part, :], got_ref[rows, 2 * part + 1, :]
            for ze in range(6):
                moved = turn(low if ze < 4 else high, 32 * (r - ze % 4))
                inner[ze] = jnp.where(lane // 32 == r, moved, inner[ze])
            rims = jnp.where(lane // 16 == r, turn(high, 16 * r - 64), rims)
        for ze in range(6):
            where = slice(192 * part + 32 * ze, 192 * part + 32 * ze + 32)
            for k, v in enumerate((inner[ze], jnp.where(lane % 8 == ze, rims, 0.0))):
                hi, lo = split(v)
                lhs_ref[0, where, 128 * k : 128 * k + 128] = hi
                lhs_ref[1, where, 128 * k : 128 * k + 128] = lo
    u = dot3((lhs_ref[0], lhs_ref[1]), (ey[0][...], ey[1][...]))
    re_c, re_s, im_c, im_s = u[:192, :256], u[:192, 256:], u[192:, :256], u[192:, 256:]
    ezs = (ez[0][...], ez[1][...])

    def forward(real, imag):
        v = dot3(ezs, split(jnp.concatenate([real, imag], axis=1)))
        return v[:256, :256] + v[256:, 256:], v[:256, 256:] - v[256:, :256]

    @pl.when(first)
    def _():
        s_ref[0], s_ref[1] = forward(re_c, -re_s)
        s_ref[2], s_ref[3] = forward(im_c, -im_s)

    @pl.when(jnp.logical_not(first))
    def _():
        s_ref[0], s_ref[1] = forward(re_c + im_s, im_c - re_s)


def back_into(a, h_ref, s_ref, q_ref, zt, ey, out_ref, at, rim_ref, first):
    a_re = s_ref[0] * h_ref[a, 0] - s_ref[1] * h_ref[a, 1]
    a_im = s_ref[0] * h_ref[a, 1] + s_ref[1] * h_ref[a, 0]
    q_ref[0], q_ref[1] = a_re, a_im

    @pl.when(first)
    def _():
        b_re = s_ref[2] * h_ref[a, 2] - s_ref[3] * h_ref[a, 3]
        b_im = s_ref[2] * h_ref[a, 3] + s_ref[3] * h_ref[a, 2]
        q_ref[0] = q_ref[0] - b_im
        q_ref[1] = q_ref[1] + b_re

    q = split(jnp.concatenate([q_ref[0], q_ref[1]], axis=1))
    v = dot3((zt[0][...], zt[1][...]), q)
    v = split(jnp.concatenate([v[:192, :256] - v[192:, 256:], v[:192, 256:] + v[192:, :256]], axis=0))
    cos = dot3(v, (ey[0][:, :256], ey[1][:, :256]), ((1,), (1,)))
    sin = dot3(v, (ey[0][:, 256:], ey[1][:, 256:]), ((1,), (1,)))
    w = (cos[:192] - sin[192:], cos[192:] + sin[:192])
    lane = lanes(N_COL)
    rims = []
    for part in range(2):
        rim = jnp.zeros((N_COL, 128), F32)
        for ze in range(6):
            rim = jnp.where(lane % 8 == ze, w[part][32 * ze : 32 * ze + 32, 128:], rim)
        rims.append(rim)
    for r in range(N_ROW):
        rows = slice(32 * r, 32 * r + 32)
        shared = jnp.zeros((N_COL, 128), F32)
        for part in range(2):
            mine = jnp.zeros((N_COL, 128), F32)
            for ze in range(6):
                to = ze if ze < 4 else ze - 4 + 2 * part
                moved = turn(w[part][32 * ze : 32 * ze + 32, :128], 32 * (to - r))
                if ze < 4:
                    mine = jnp.where(lane // 32 == to, moved, mine)
                else:
                    shared = jnp.where(lane // 32 == to, moved, shared)
            out_ref[rows, at + part, :] = mine
            to = 2 * a + part
            old = rim_ref[rows]
            rim_ref[rows] = jnp.where(lane // 16 == to, turn(rims[part], 16 * (to - r)), old)
        out_ref[rows, at + 2, :] = shared


MESH = pl.DeviceIdType.MESH
N_IN = 21


def field_kernel(*refs, n):
    hbm, (ft_ref, f8_ref, scale_ref, moved_ref) = refs[:N_IN], refs[N_IN : N_IN + 4]
    held = refs[N_IN + 4 : 2 * N_IN + 4]
    (lhs_p, pack_s, pack_r, a_ref, b_ref, acc_ref, send1, recv1, h_ref, lhs_f, s_ref, q_ref, *late) = refs[
        2 * N_IN + 4 : 2 * N_IN + 21
    ]
    send2, recv2, rim_ref = late[:2], late[2:4], late[4]
    meet, in_sem, own_sem, ss_m, rs_m, ss_1, rs_1, ss_2, rs_2 = refs[2 * N_IN + 21 :]
    row, col = lax.axis_index("row"), lax.axis_index("col")
    me = row * N_COL + col
    first = me == 0

    def device(d):
        return (d >> 5, d & 31)

    copies = [pltpu.make_async_copy(h, v, in_sem.at[i]) for i, (h, v) in enumerate(zip(hbm, held))]
    for copy in copies:
        copy.start()

    barrier = pltpu.get_barrier_semaphore()

    def greet_row(sem):
        for i in range(1, N_ROW):
            pl.semaphore_signal(sem, inc=1, device_id=((row + i) & 3, col), device_id_type=MESH)

    def greet_col(i, _):
        pl.semaphore_signal(barrier, inc=1, device_id=(row, (col + i) & 31), device_id_type=MESH)
        return 0

    greet_row(barrier)
    lax.fori_loop(1, N_COL, greet_col, 0)
    acc_ref[...] = jnp.zeros_like(acc_ref)

    for copy in copies[:6]:
        copy.wait()
    pack_into(*held[:6], lhs_p, pack_s)
    for copy in copies[6:10]:
        copy.wait()
    cell_ref, corner_ref, frac_ref, q_in = held[6:10]
    blk = a_ref.shape[1]
    steps = cell_ref.shape[1] // blk

    def resident(i, _):
        def rows(s):
            here = pl.ds(pl.multiple_of(i * blk + s * n, n), n)
            return (
                cell_ref[:, here],
                corner_ref[:, here],
                frac_ref[0:1, here],
                frac_ref[1:2, here],
                frac_ref[2:3, here],
                q_in[:, here],
            )

        deposit_block(rows, a_ref, b_ref, acc_ref, n)
        return 0

    lax.fori_loop(0, steps // 2, resident, 0)
    pl.semaphore_wait(barrier, N_ROW - 1 + N_COL - 1)
    greet_row(meet)

    def send_migrants(i, _):
        c = (col + i) & 31
        pltpu.make_async_remote_copy(
            src_ref=pack_s.at[c],
            dst_ref=pack_r.at[col],
            send_sem=ss_m,
            recv_sem=rs_m,
            device_id=(row, c),
            device_id_type=MESH,
        ).start()
        return 0

    lax.fori_loop(1, N_COL, send_migrants, 0)
    own = pltpu.make_async_copy(pack_s.at[col], pack_r.at[col], own_sem.at[0])
    own.start()
    lax.fori_loop(steps // 2, steps, resident, 0)
    own.wait()
    rest = pl.ds(0, N_COL - 1)
    pltpu.make_async_remote_copy(
        src_ref=pack_s.at[rest],
        dst_ref=pack_r.at[rest],
        send_sem=ss_m,
        recv_sem=rs_m,
        device_id=(row, col),
        device_id_type=MESH,
    ).wait()
    for s in range(N_COL):
        moved_ref[:, 128 * s : 128 * s + 128] = pack_r[s]

    def migrant(i, _):
        def rows(s):
            here = pl.ds(pl.multiple_of(i * blk + s * n, n), n)
            got = moved_ref[:, here]
            return (
                got[7:8].astype(I32),
                got[8:9].astype(I32),
                got[0:1],
                got[1:2],
                got[2:3],
                got[3:4],
            )

        deposit_block(rows, a_ref, b_ref, acc_ref, n)
        return 0

    lax.fori_loop(0, moved_ref.shape[1] // blk, migrant, 0)
    for copy in copies[10:]:
        copy.wait()
    green_ref = held[10]
    ey, ez, zt, dx, xi = (held[11 + 2 * i : 13 + 2 * i] for i in range(5))

    acc = acc_ref[...]
    grid = (acc[:ROWS, :128] + acc[ROWS:, 128:]) + (acc[:ROWS, 128:] + acc[ROWS:, :128])
    sent = dot3((dx[0][...], dx[1][...]), split(grid), ((1,), (1,)))
    sent = jnp.concatenate([sent, jnp.zeros((256, PAD - ROWS), F32)], axis=1)
    for part in range(2):
        for half in range(2):
            send1[:, 2 * part + half, :] = sent[128 * part : 128 * part + 128, 128 * half : 128 * half + 128]

    def exchange(src, dst, ss, rs, own_at):
        def go(i, _):
            d = (me + i) & 127
            pltpu.make_async_remote_copy(
                src_ref=src.at[d],
                dst_ref=dst.at[me],
                send_sem=ss,
                recv_sem=rs,
                device_id=device(d),
                device_id_type=MESH,
            ).start()
            return 0

        lax.fori_loop(1, SLOTS, go, 0)
        own = pltpu.make_async_copy(src.at[me], dst.at[me], own_at)
        own.start()
        return own

    def finish(own, src, dst, ss, rs):
        own.wait()
        rest = pl.ds(0, SLOTS - 1)
        pltpu.make_async_remote_copy(
            src_ref=src.at[rest],
            dst_ref=dst.at[rest],
            send_sem=ss,
            recv_sem=rs,
            device_id=(row, col),
            device_id_type=MESH,
        ).wait()

    pl.semaphore_wait(meet, N_ROW - 1)
    own = exchange(send1, recv1, ss_1, rs_1, own_sem.at[1])
    green_into(green_ref, h_ref, first)
    finish(own, send1, recv1, ss_1, rs_1)
    forward_into(recv1, ey, ez, lhs_f, s_ref, first)
    rim_ref[...] = jnp.zeros_like(rim_ref)
    back_into(0, h_ref, s_ref, q_ref, zt, ey, send2[0], 0, rim_ref, first)
    back_into(1, h_ref, s_ref, q_ref, zt, ey, send2[0], 3, rim_ref, first)
    owns = [exchange(send2[0], recv2[0], ss_2.at[0], rs_2.at[0], own_sem.at[2])]
    back_into(2, h_ref, s_ref, q_ref, zt, ey, send2[1], 0, rim_ref, first)
    send2[1][:, 3, :] = rim_ref[...]
    owns.append(exchange(send2[1], recv2[1], ss_2.at[1], rs_2.at[1], own_sem.at[3]))
    for k in range(2):
        finish(owns[k], send2[k], recv2[k], ss_2.at[k], rs_2.at[k])
    lane = lanes(SLOTS)
    rims = recv2[1][:, 3, :]
    for a in range(3):
        from_ref, at = recv2[a // 2], 3 * (a % 2)
        shared = from_ref[:, at + 2, :]
        parts = []
        for part in range(2):
            rest = jnp.where(lane < 80, turn(rims, 64 - 16 * (2 * a + part)), 0.0)
            rest = jnp.where(lane < 64, turn(shared, -64 * part), rest)
            parts.append(jnp.concatenate([from_ref[:, at + part, :], rest], axis=1))
        field = dot3((xi[0][...], xi[1][...]), split(jnp.concatenate(parts, axis=0)))
        top = jnp.max(jnp.max(jnp.abs(field), axis=0, keepdims=True), axis=1, keepdims=True)
        top = jnp.maximum(top, 1e-30)
        field = field / top
        hi = field.astype(BF).astype(F32)
        here = slice(128 * a, 128 * a + 128)
        ft_ref[here] = (hi * 65536.0).astype(BF)
        f8_ref[here, :PAD] = ((field - hi) * 65536.0).astype(F8)
        f8_ref[here, PAD:] = (hi * 16.0).astype(F8)
        scale_ref[a : a + 1] = jnp.broadcast_to(top * (1.0 / 65536.0), (1, 128))
    scale_ref[3:] = jnp.zeros((5, 128), F32)


def field_of(operands, blk=4096, n=512):
    ops = [o.reshape(1, -1) if o.ndim == 1 else o for o in operands]
    assert len(ops) == N_IN
    cap = 128
    dma = pltpu.SemaphoreType.DMA
    return pl.pallas_call(
        functools.partial(field_kernel, n=n),
        name="field",
        out_shape=(
            jax.ShapeDtypeStruct((384, PAD), BF),
            jax.ShapeDtypeStruct((384, 2 * PAD), F8),
            jax.ShapeDtypeStruct((8, 128), F32),
            jax.ShapeDtypeStruct((9, N_COL * cap), F32),
        ),
        in_specs=[pl.BlockSpec(memory_space=pltpu.MemorySpace.HBM)] * N_IN,
        out_specs=(pl.BlockSpec(memory_space=pltpu.VMEM),) * 4,
        scratch_shapes=[pltpu.VMEM(o.shape, o.dtype) for o in ops]
        + [
            pltpu.VMEM((3 * 512, ops[0].shape[1]), BF),
            pltpu.VMEM((N_COL, 9, cap), F32),
            pltpu.VMEM((N_COL, 9, cap), F32),
            pltpu.VMEM((2 * ROWS, blk), BF),
            pltpu.VMEM((256, blk), BF),
            pltpu.VMEM((2 * ROWS, 256), F32),
            pltpu.VMEM((SLOTS, 4, 128), F32),
            pltpu.VMEM((SLOTS, 4, 128), F32),
            pltpu.VMEM((3, 4, 256, 256), F32),
            pltpu.VMEM((2, 384, PAD), BF),
            pltpu.VMEM((4, 256, 256), F32),
            pltpu.VMEM((2, 256, 256), F32),
            pltpu.VMEM((SLOTS, 6, 128), F32),
            pltpu.VMEM((SLOTS, 4, 128), F32),
            pltpu.VMEM((SLOTS, 6, 128), F32),
            pltpu.VMEM((SLOTS, 4, 128), F32),
            pltpu.VMEM((SLOTS, 128), F32),
            pltpu.SemaphoreType.REGULAR,
            dma((N_IN,)),
            dma((5,)),
            dma(()),
            dma(()),
            dma(()),
            dma(()),
            dma((2,)),
            dma((2,)),
        ],
        compiler_params=pltpu.CompilerParams(vmem_limit_bytes=BIG, has_side_effects=True, collective_id=0),
    )(*ops)


def body(
    resident_cell,
    resident_corner,
    resident_frac,
    resident_charge,
    resident_momentum,
    migrant_dest,
    migrant_cell,
    migrant_corner,
    migrant_frac,
    migrant_charge,
    migrant_momentum,
    green,
):
    consts = [jnp.asarray(t) for pair in tables() for t in pair]
    stayed = (resident_cell, resident_corner, resident_frac, resident_charge)
    *field, moved = field_of(
        [
            migrant_dest.reshape(-1),
            migrant_cell,
            migrant_corner,
            migrant_frac,
            migrant_charge,
            migrant_momentum,
            *stayed,
            green,
            *consts,
        ]
    )
    return kick(field, moved, *stayed, resident_momentum)


def solution(mesh):
    both = ("row", "col")
    in_specs = (
        P(both),
        P(both),
        P(None, both),
        P(both),
        P(None, both),
        P(both, None),
        P(both),
        P(both),
        P(None, both),
        P(both),
        P(None, both),
        P(None, None, both, None, None),
    )
    out_specs = (P(None, both), P(None, both))
    return jax.shard_map(body, mesh=mesh, in_specs=in_specs, out_specs=out_specs, check_vma=False)
```

```python
import functools

import jax
import jax.numpy as jnp
import numpy as np
from jax import lax
from jax.experimental import pallas as pl
from jax.experimental.pallas import tpu as pltpu
from jax.sharding import PartitionSpec as P

F32, BF, I32, F8 = jnp.float32, jnp.bfloat16, jnp.int32, jnp.float8_e4m3fn
N_ROW, N_COL = 4, 32
SLOTS = N_ROW * N_COL
ROWS = 208
PAD = 256
BIG = 60 << 20


def split_np(table):
    hi = table.astype(jnp.bfloat16)
    return hi, (table - hi.astype(np.float64)).astype(jnp.bfloat16)


def y_places():
    y = np.full(PAD, -1)
    y[:128] = np.arange(128)
    for r in range(N_ROW):
        for side in range(2):
            first = 128 + 16 * r + 8 * side
            y[first : first + 6] = 32 * r + 33 * side - 1
    return y


def tables():
    wave = np.arange(256)
    y = y_places()[:, None]
    angle = 2 * np.pi / 256 * (y * wave % 256)
    live = (y >= 0) & (y < 128)
    ey = np.concatenate([np.cos(angle), np.sin(angle)], axis=1) * live
    zg = (4 * np.arange(N_COL)[None] + np.arange(6)[:, None] - 1).reshape(-1)
    live = ((zg >= 0) & (zg < 128))[None]
    angle = 2 * np.pi / 256 * (wave[:, None] * zg % 256)
    ez = np.stack([np.cos(angle) * live, np.sin(angle) * live])
    ezt = ez.transpose(0, 2, 1).reshape(384, 256)
    x, j = np.arange(128), np.arange(128)
    angle = 2 * np.pi / 256 * (j[:, None] * x % 256)
    imag = -np.sin(angle)
    imag[0] = 1 - 2 * (x % 2)
    dx = np.concatenate([np.cos(angle), imag])
    return [split_np(t) for t in (ey, ez.reshape(512, 192), ezt, dx, dx.T / 256.0**3)]


def split(v):
    hi = v.astype(BF)
    return hi, (v - hi.astype(F32)).astype(BF)


def dot3(a, b, dims=((1,), (0,))):
    one = lambda p, q: lax.dot_general(p, q, (dims, ((), ())), preferred_element_type=F32)
    return one(a[0], b[0]) + (one(a[0], b[1]) + one(a[1], b[0]))


def tile16(row, n):
    return jnp.broadcast_to(row, (16, n)).astype(BF)


def yz_weights(cell, corner, fy, fz, q, n, write):
    y = (cell >> 7) & 31
    z = (cell >> 12) + 1
    yfar = y + ((corner >> 1) & 1) * 2 - 1
    zfar = z + ((corner >> 2) & 1) * 2 - 1
    io8 = lax.broadcasted_iota(I32, (8, n), 0)
    wz = jnp.where(io8 == z, (1.0 - fz) * q, jnp.where(io8 == zfar, fz * q, 0.0))
    near = wz * (1.0 - fy)
    far = wz * fy
    nh = near.astype(BF).astype(F32); nl = near - nh
    fh = far.astype(BF).astype(F32); fl = far - fh
    io16 = lax.broadcasted_iota(I32, (16, n), 0).astype(BF)
    yb = jnp.broadcast_to(y.astype(F32), (16, n)).astype(BF)
    yfb = jnp.broadcast_to(yfar.astype(F32), (16, n)).astype(BF)
    zero = jnp.zeros((16, n), BF)
    masks = [(yb == io16, yfb == io16), (yb == io16 + 16.0, yfb == io16 + 16.0)]
    for ze in range(6):
        a, b, c, d = (tile16(v[ze:ze+1], n) for v in (nh, fh, nl, fl))
        for h in range(2):
            mn, mf = masks[h]
            write(ze*32 + h*16, jnp.where(mn, a, jnp.where(mf, b, zero)), jnp.where(mn, c, jnp.where(mf, d, zero)))
    isb = yfar < 0
    isa = yfar > 31
    rh = jnp.concatenate([jnp.where(isb, fh, 0.0), jnp.where(isa, fh, 0.0)], axis=0).astype(BF)
    rl = jnp.concatenate([jnp.where(isb, fl, 0.0), jnp.where(isa, fl, 0.0)], axis=0).astype(BF)
    write(192, rh, rl)

def x_weights(cell, corner, fx, n, write):
    x = cell & 127
    xfar = x + (corner & 1) * 2 - 1
    gx = 1.0 - fx
    gh = gx.astype(BF).astype(F32)
    fh = fx.astype(BF).astype(F32)
    gh, gl, fh, fl = (tile16(v, n) for v in (gh, gx - gh, fh, fx - fh))
    io16 = lax.broadcasted_iota(I32, (16, n), 0).astype(BF)
    xb, xfb = tile16(x.astype(F32), n), tile16(xfar.astype(F32), n)
    zero = jnp.zeros((16, n), BF)
    for t in range(8):
        near, far = xb == io16 + BF(16 * t), xfb == io16 + BF(16 * t)
        write(16 * t, jnp.where(near, gh, jnp.where(far, fh, zero)), jnp.where(near, gl, jnp.where(far, fl, zero)))


def deposit_block(rows, a_ref, b_ref, acc_ref, n):
    for s in range(a_ref.shape[1] // n):
        here = pl.ds(s * n, n)
        cell, corner, fx, fy, fz, q = rows(s)

        def write_a(r, hi, lo):
            a_ref[r : r + 16, here] = hi
            a_ref[ROWS + r : ROWS + r + 16, here] = lo

        def write_b(r, hi, lo):
            b_ref[r : r + 16, here] = hi
            b_ref[128 + r : 128 + r + 16, here] = lo

        yz_weights(cell, corner, fy, fz, q, n, write_a)
        x_weights(cell, corner, fx, n, write_b)
    acc_ref[...] += lax.dot_general(a_ref[...], b_ref[...], (((1,), (1,)), ((), ())), preferred_element_type=F32)


def pack_into(dest_ref, cell_ref, corner_ref, frac_ref, q_ref, mom_ref, lhs_ref, out_ref):
    total = dest_ref.shape[-1]
    dest = dest_ref[...]
    hits = (lax.broadcasted_iota(I32, (N_COL, total), 0) == dest).astype(F32)
    upper = (lax.broadcasted_iota(I32, (256, 256), 0) < lax.broadcasted_iota(I32, (256, 256), 1)).astype(BF)
    carry = jnp.zeros((N_COL, 1), F32)
    ranks = []
    for s in range(0, total, 256):
        part = hits[:, s : s + 256]
        before = jnp.dot(part.astype(BF), upper, preferred_element_type=F32) + carry
        carry = carry + jnp.sum(part, axis=1, keepdims=True)
        ranks.append(jnp.sum(part * before, axis=0, keepdims=True))
    rank = jnp.concatenate(ranks, axis=1)
    cap = out_ref.shape[-1]
    choose = (lax.broadcasted_iota(I32, (cap, total), 0).astype(F32) == rank).astype(BF)
    payload = jnp.concatenate(
        [
            frac_ref[...],
            q_ref[...],
            mom_ref[...],
            cell_ref[...].astype(F32),
            corner_ref[...].astype(F32),
            jnp.zeros((7, total), F32),
        ],
        axis=0,
    )
    hi = payload.astype(BF)
    rest = payload - hi.astype(F32)
    mid = rest.astype(BF)
    low = (rest - mid.astype(F32)).astype(BF)
    destb = tile16(dest.astype(F32), total)
    zero = jnp.zeros((16, total), BF)
    for d in range(N_COL):
        mask = destb == BF(d)
        for i, piece in enumerate((hi, mid, low)):
            lhs_ref[i * 512 + d * 16 : i * 512 + d * 16 + 16] = jnp.where(mask, piece, zero)
    got = lax.dot_general(lhs_ref[...], choose, (((1,), (1,)), ((), ())), preferred_element_type=F32)
    got = (got[:512] + got[512:1024]) + got[1024:]
    for d in range(N_COL):
        out_ref[d] = got[d * 16 : d * 16 + 9]


def yz_tiles(cell, corner, fy, fz, q, n, write):
    y = (cell >> 7) & 31
    z = (cell >> 12) + 1
    yfar = y + ((corner >> 1) & 1) * 2 - 1
    zfar = z + ((corner >> 2) & 1) * 2 - 1
    io8 = lax.broadcasted_iota(I32, (8, n), 0)
    wz = jnp.where(io8 == z, (1.0 - fz) * q, jnp.where(io8 == zfar, fz * q, 0.0))
    near = wz * (1.0 - fy)
    far = wz * fy
    nh = near.astype(BF).astype(F32)
    fh = far.astype(BF).astype(F32)
    nl, fl = (near - nh) * 4096.0, (far - fh) * 4096.0

    def big(row):
        half = tile16(row, n)
        return jnp.concatenate([half, half], axis=0)

    io = lax.broadcasted_iota(I32, (32, n), 0).astype(F32).astype(BF)
    at_near, at_far = big(y.astype(F32)) == io, big(yfar.astype(F32)) == io
    zero = jnp.zeros((32, n), BF)
    for ze in range(6):
        a, b, c, d = (big(v[ze : ze + 1]) for v in (nh, fh, nl, fl))
        write(ze * 32, jnp.where(at_near, a, jnp.where(at_far, b, zero)), jnp.where(at_near, c, jnp.where(at_far, d, zero)))
    below, above = yfar < 0, yfar > 31
    rims = [
        jnp.concatenate([jnp.where(below, v, 0.0), jnp.where(above, v, 0.0), jnp.zeros((16, n), F32)], axis=0)
        for v in (fh, fl)
    ]
    write(192, rims[0].astype(BF), rims[1].astype(BF))


def kick_chunk(ft_ref, f8_ref, w_ref, w8_ref, here, n, rows):
    cell, corner, fx, fy, fz, q = rows

    def write(r, hi, lo):
        w_ref[r : r + 32, here] = hi
        w8_ref[r : r + 32, here] = hi.astype(F8)
        w8_ref[PAD + r : PAD + r + 32, here] = lo.astype(F8)

    yz_tiles(cell, corner, fy, fz, q, n, write)
    got = jnp.dot(ft_ref[...], w_ref[:, here], preferred_element_type=F32)
    more = jnp.dot(f8_ref[...], w8_ref[:, here], preferred_element_type=F32)
    x = cell & 127
    xfar = x + (corner & 1) * 2 - 1
    io = lax.broadcasted_iota(I32, (128, n), 0)
    wx = jnp.where(io == x, 1.0 - fx, jnp.where(io == xfar, fx, 0.0))
    total = got + more
    return [jnp.sum(total[a * 128 : a * 128 + 128] * wx, axis=0, keepdims=True) for a in range(3)]


def kick_kernel(*refs, n):
    hbm, (out_hbm, migrant_hbm), held = refs[:9], refs[9:11], refs[11:20]
    out_ref, migrant_ref, w_ref, w8_ref, made_sem, in_sem, out_sem, migrant_sem = refs[20:]
    made = [pltpu.make_async_copy(hbm[i], held[i], made_sem.at[i]) for i in range(4)]
    for copy in made:
        copy.start()
    (ft_ref, f8_ref, scale_ref, moved_ref), hbm, held = held[:4], hbm[4:], held[4:]
    cell_ref, corner_ref, frac_ref, q_ref, mom_ref = held
    blk = w_ref.shape[1]
    total = cell_ref.shape[1]
    pieces = (pl.ds(0, blk), pl.ds(blk, total - blk))
    copies = [
        [pltpu.make_async_copy(h.at[:, p], v.at[:, p], in_sem.at[j, i]) for i, (h, v) in enumerate(zip(hbm, held))]
        for j, p in enumerate(pieces)
    ]
    for copy in copies[0] + copies[1]:
        copy.start()
    for r in (224, 480):
        w8_ref[r : r + 32] = jnp.zeros((32, blk), F8)
    w_ref[224:] = jnp.zeros((32, blk), BF)
    chunk = functools.partial(kick_chunk, ft_ref, f8_ref, w_ref, w8_ref)
    for copy in made:
        copy.wait()

    def migrants(i, _):
        for s in range(blk // n):
            here = pl.ds(pl.multiple_of(i * blk + s * n, n), n)
            got = moved_ref[:, here]
            rows = (got[7:8].astype(I32), got[8:9].astype(I32), got[0:1], got[1:2], got[2:3], got[3:4])
            kicks = chunk(pl.ds(s * n, n), n, rows)
            for a in range(3):
                migrant_ref[a : a + 1, here] = got[4 + a : 5 + a] + kicks[a] * scale_ref[a : a + 1, 0:1]
        return 0

    lax.fori_loop(0, moved_ref.shape[1] // blk, migrants, 0)
    migrant_out = pltpu.make_async_copy(migrant_ref, migrant_hbm, migrant_sem)
    migrant_out.start()
    for copy in copies[0]:
        copy.wait()

    def residents(i, _):
        @pl.when(i == 1)
        def _():
            for copy in copies[1]:
                copy.wait()

        for s in range(blk // n):
            here = pl.ds(pl.multiple_of(i * blk + s * n, n), n)
            rows = (
                cell_ref[:, here],
                corner_ref[:, here],
                frac_ref[0:1, here],
                frac_ref[1:2, here],
                frac_ref[2:3, here],
                q_ref[:, here],
            )
            kicks = chunk(pl.ds(s * n, n), n, rows)
            for a in range(3):
                out_ref[a : a + 1, here] = mom_ref[a : a + 1, here] + kicks[a] * scale_ref[a : a + 1, 0:1]
        block = pl.ds(pl.multiple_of(i * blk, blk), blk)
        pltpu.make_async_copy(out_ref.at[:, block], out_hbm.at[:, block], out_sem).start()
        return 0

    lax.fori_loop(0, total // blk, residents, 0)
    migrant_out.wait()
    pltpu.make_async_copy(out_ref, out_hbm, out_sem).wait()


def kick(tables_of, moved, cell, corner, frac, q, mom, blk=4096, n=256):
    ops = [*tables_of, moved, cell.reshape(1, -1), corner.reshape(1, -1), frac, q.reshape(1, -1), mom]
    hbm = pl.BlockSpec(memory_space=pltpu.MemorySpace.HBM)
    return pl.pallas_call(
        functools.partial(kick_kernel, n=n),
        name="kick",
        out_shape=(jax.ShapeDtypeStruct(mom.shape, F32), jax.ShapeDtypeStruct((3, moved.shape[1]), F32)),
        in_specs=[hbm] * 9,
        out_specs=(hbm, hbm),
        scratch_shapes=[pltpu.VMEM(o.shape, o.dtype) for o in ops]
        + [
            pltpu.VMEM(mom.shape, F32),
            pltpu.VMEM((3, moved.shape[1]), F32),
            pltpu.VMEM((PAD, blk), BF),
            pltpu.VMEM((2 * PAD, blk), F8),
            pltpu.SemaphoreType.DMA((4,)),
            pltpu.SemaphoreType.DMA((2, 5)),
            pltpu.SemaphoreType.DMA(()),
            pltpu.SemaphoreType.DMA(()),
        ],
        compiler_params=pltpu.CompilerParams(vmem_limit_bytes=BIG),
    )(*ops)


def green_into(green_ref, h_ref, first):
    index = lax.broadcasted_iota(I32, (256, 256), 0) + lax.broadcasted_iota(I32, (256, 256), 1)
    mirror = ((index == 0) | (index == 256)).astype(BF)

    def flip(plane):
        half = jnp.dot(mirror, plane, preferred_element_type=F32).astype(BF)
        return jnp.dot(half, mirror, preferred_element_type=F32)

    @pl.when(first)
    def _():
        for a in range(3):
            for sign in range(2):
                real, imag = green_ref[a, 0, sign], green_ref[a, 1, sign]
                h_ref[a, 2 * sign] = 0.5 * (real.astype(F32) + flip(real))
                h_ref[a, 2 * sign + 1] = 0.5 * (imag.astype(F32) - flip(imag))

    @pl.when(jnp.logical_not(first))
    def _():
        for a in range(3):
            h_ref[a, 0] = green_ref[a, 0, 0].astype(F32) + flip(green_ref[a, 0, 1])
            h_ref[a, 1] = green_ref[a, 1, 0].astype(F32) - flip(green_ref[a, 1, 1])


def lanes(rows):
    return lax.broadcasted_iota(I32, (rows, 128), 1)


def turn(v, by):
    by = by % 128
    return pltpu.roll(v, by, 1) if by else v


def forward_into(got_ref, ey, ez, lhs_ref, s_ref, first):
    lane = lanes(N_COL)
    for part in range(2):
        inner = [jnp.zeros((N_COL, 128), F32)] * 6
        rims = jnp.zeros((N_COL, 128), F32)
        for r in range(N_ROW):
            rows = slice(32 * r, 32 * r + 32)
            low, high = got_ref[rows, 2 * part, :], got_ref[rows, 2 * part + 1, :]
            for ze in range(6):
                moved = turn(low if ze < 4 else high, 32 * (r - ze % 4))
                inner[ze] = jnp.where(lane // 32 == r, moved, inner[ze])
            rims = jnp.where(lane // 16 == r, turn(high, 16 * r - 64), rims)
        for ze in range(6):
            where = slice(192 * part + 32 * ze, 192 * part + 32 * ze + 32)
            for k, v in enumerate((inner[ze], jnp.where(lane % 8 == ze, rims, 0.0))):
                hi, lo = split(v)
                lhs_ref[0, where, 128 * k : 128 * k + 128] = hi
                lhs_ref[1, where, 128 * k : 128 * k + 128] = lo
    u = dot3((lhs_ref[0], lhs_ref[1]), (ey[0][...], ey[1][...]))
    re_c, re_s, im_c, im_s = u[:192, :256], u[:192, 256:], u[192:, :256], u[192:, 256:]
    ezs = (ez[0][...], ez[1][...])

    def forward(real, imag):
        v = dot3(ezs, split(jnp.concatenate([real, imag], axis=1)))
        return v[:256, :256] + v[256:, 256:], v[:256, 256:] - v[256:, :256]

    @pl.when(first)
    def _():
        s_ref[0], s_ref[1] = forward(re_c, -re_s)
        s_ref[2], s_ref[3] = forward(im_c, -im_s)

    @pl.when(jnp.logical_not(first))
    def _():
        s_ref[0], s_ref[1] = forward(re_c + im_s, im_c - re_s)


def back_into(a, h_ref, s_ref, q_ref, zt, ey, out_ref, at, rim_ref, first):
    a_re = s_ref[0] * h_ref[a, 0] - s_ref[1] * h_ref[a, 1]
    a_im = s_ref[0] * h_ref[a, 1] + s_ref[1] * h_ref[a, 0]
    q_ref[0], q_ref[1] = a_re, a_im

    @pl.when(first)
    def _():
        b_re = s_ref[2] * h_ref[a, 2] - s_ref[3] * h_ref[a, 3]
        b_im = s_ref[2] * h_ref[a, 3] + s_ref[3] * h_ref[a, 2]
        q_ref[0] = q_ref[0] - b_im
        q_ref[1] = q_ref[1] + b_re

    q = split(jnp.concatenate([q_ref[0], q_ref[1]], axis=1))
    v = dot3((zt[0][...], zt[1][...]), q)
    v = split(jnp.concatenate([v[:192, :256] - v[192:, 256:], v[:192, 256:] + v[192:, :256]], axis=0))
    cos = dot3(v, (ey[0][:, :256], ey[1][:, :256]), ((1,), (1,)))
    sin = dot3(v, (ey[0][:, 256:], ey[1][:, 256:]), ((1,), (1,)))
    w = (cos[:192] - sin[192:], cos[192:] + sin[:192])
    lane = lanes(N_COL)
    rims = []
    for part in range(2):
        rim = jnp.zeros((N_COL, 128), F32)
        for ze in range(6):
            rim = jnp.where(lane % 8 == ze, w[part][32 * ze : 32 * ze + 32, 128:], rim)
        rims.append(rim)
    for r in range(N_ROW):
        rows = slice(32 * r, 32 * r + 32)
        shared = jnp.zeros((N_COL, 128), F32)
        for part in range(2):
            mine = jnp.zeros((N_COL, 128), F32)
            for ze in range(6):
                to = ze if ze < 4 else ze - 4 + 2 * part
                moved = turn(w[part][32 * ze : 32 * ze + 32, :128], 32 * (to - r))
                if ze < 4:
                    mine = jnp.where(lane // 32 == to, moved, mine)
                else:
                    shared = jnp.where(lane // 32 == to, moved, shared)
            out_ref[rows, at + part, :] = mine
            to = 2 * a + part
            old = rim_ref[rows]
            rim_ref[rows] = jnp.where(lane // 16 == to, turn(rims[part], 16 * (to - r)), old)
        out_ref[rows, at + 2, :] = shared


MESH = pl.DeviceIdType.MESH
N_IN = 21


def field_kernel(*refs, n):
    hbm, (ft_out, f8_out, scale_out, moved_out) = refs[:N_IN], refs[N_IN : N_IN + 4]
    held = refs[N_IN + 4 : 2 * N_IN + 4]
    (lhs_p, pack_s, pack_r, a_ref, b_ref, acc_ref, send1, recv1, h_ref, lhs_f, s_ref, q_ref, *late) = refs[
        2 * N_IN + 4 : 2 * N_IN + 25
    ]
    send2, recv2, rim_ref = late[:2], late[2:4], late[4]
    ft_ref, f8_ref, scale_ref, moved_ref = late[5:]
    meet, in_sem, own_sem, ss_m, rs_m, ss_1, rs_1, ss_2, rs_2, out_sem = refs[2 * N_IN + 25 :]
    row, col = lax.axis_index("row"), lax.axis_index("col")
    me = row * N_COL + col
    first = me == 0

    def device(d):
        return (d >> 5, d & 31)

    copies = [pltpu.make_async_copy(h, v, in_sem.at[i]) for i, (h, v) in enumerate(zip(hbm, held))]
    for copy in copies[:6]:
        copy.start()

    barrier = pltpu.get_barrier_semaphore()

    def greet_row(sem):
        for i in range(1, N_ROW):
            pl.semaphore_signal(sem, inc=1, device_id=((row + i) & 3, col), device_id_type=MESH)

    def greet_col(i, _):
        pl.semaphore_signal(barrier, inc=1, device_id=(row, (col + i) & 31), device_id_type=MESH)
        return 0

    greet_row(barrier)
    lax.fori_loop(1, N_COL, greet_col, 0, unroll=8)
    for copy in copies[6:]:
        copy.start()
    acc_ref[...] = jnp.zeros_like(acc_ref)

    for copy in copies[:6]:
        copy.wait()
    pack_into(*held[:6], lhs_p, pack_s)
    for copy in copies[6:10]:
        copy.wait()
    cell_ref, corner_ref, frac_ref, q_in = held[6:10]
    blk = a_ref.shape[1]
    steps = cell_ref.shape[1] // blk

    def resident(i, _):
        def rows(s):
            here = pl.ds(pl.multiple_of(i * blk + s * n, n), n)
            return (
                cell_ref[:, here],
                corner_ref[:, here],
                frac_ref[0:1, here],
                frac_ref[1:2, here],
                frac_ref[2:3, here],
                q_in[:, here],
            )

        deposit_block(rows, a_ref, b_ref, acc_ref, n)
        return 0

    lax.fori_loop(0, steps // 2, resident, 0)
    pl.semaphore_wait(barrier, N_ROW - 1 + N_COL - 1)
    greet_row(meet)

    def send_migrants(i, _):
        c = (col + i) & 31
        pltpu.make_async_remote_copy(
            src_ref=pack_s.at[c],
            dst_ref=pack_r.at[col],
            send_sem=ss_m,
            recv_sem=rs_m,
            device_id=(row, c),
            device_id_type=MESH,
        ).start()
        return 0

    lax.fori_loop(1, N_COL, send_migrants, 0, unroll=8)
    own = pltpu.make_async_copy(pack_s.at[col], pack_r.at[col], own_sem.at[0])
    own.start()
    lax.fori_loop(steps // 2, steps, resident, 0)
    own.wait()
    rest = pl.ds(0, N_COL - 1)
    pltpu.make_async_remote_copy(
        src_ref=pack_s.at[rest],
        dst_ref=pack_r.at[rest],
        send_sem=ss_m,
        recv_sem=rs_m,
        device_id=(row, col),
        device_id_type=MESH,
    ).wait()
    for s in range(N_COL):
        moved_ref[:, 128 * s : 128 * s + 128] = pack_r[s]
    leaving = [pltpu.make_async_copy(moved_ref, moved_out, out_sem.at[0])]
    leaving[0].start()

    def migrant(i, _):
        def rows(s):
            here = pl.ds(pl.multiple_of(i * blk + s * n, n), n)
            got = moved_ref[:, here]
            return (
                got[7:8].astype(I32),
                got[8:9].astype(I32),
                got[0:1],
                got[1:2],
                got[2:3],
                got[3:4],
            )

        deposit_block(rows, a_ref, b_ref, acc_ref, n)
        return 0

    lax.fori_loop(0, moved_ref.shape[1] // blk, migrant, 0)
    for copy in copies[10:]:
        copy.wait()
    green_ref = held[10]
    ey, ez, zt, dx, xi = (held[11 + 2 * i : 13 + 2 * i] for i in range(5))

    acc = acc_ref[...]
    grid = (acc[:ROWS, :128] + acc[ROWS:, 128:]) + (acc[:ROWS, 128:] + acc[ROWS:, :128])
    sent = dot3((dx[0][...], dx[1][...]), split(grid), ((1,), (1,)))
    sent = jnp.concatenate([sent, jnp.zeros((256, PAD - ROWS), F32)], axis=1)
    for part in range(2):
        for half in range(2):
            send1[:, 2 * part + half, :] = sent[128 * part : 128 * part + 128, 128 * half : 128 * half + 128]

    def exchange(src, dst, ss, rs, own_at):
        def go(i, _):
            d = (me + i) & 127
            pltpu.make_async_remote_copy(
                src_ref=src.at[d],
                dst_ref=dst.at[me],
                send_sem=ss,
                recv_sem=rs,
                device_id=device(d),
                device_id_type=MESH,
            ).start()
            return 0

        lax.fori_loop(1, SLOTS, go, 0, unroll=8)
        own = pltpu.make_async_copy(src.at[me], dst.at[me], own_at)
        own.start()
        return own

    def finish(own, src, dst, ss, rs):
        own.wait()
        rest = pl.ds(0, SLOTS - 1)
        pltpu.make_async_remote_copy(
            src_ref=src.at[rest],
            dst_ref=dst.at[rest],
            send_sem=ss,
            recv_sem=rs,
            device_id=(row, col),
            device_id_type=MESH,
        ).wait()

    pl.semaphore_wait(meet, N_ROW - 1)
    own = exchange(send1, recv1, ss_1, rs_1, own_sem.at[1])
    green_into(green_ref, h_ref, first)
    finish(own, send1, recv1, ss_1, rs_1)
    forward_into(recv1, ey, ez, lhs_f, s_ref, first)
    rim_ref[...] = jnp.zeros_like(rim_ref)
    back_into(0, h_ref, s_ref, q_ref, zt, ey, send2[0], 0, rim_ref, first)
    back_into(1, h_ref, s_ref, q_ref, zt, ey, send2[0], 3, rim_ref, first)
    owns = [exchange(send2[0], recv2[0], ss_2.at[0], rs_2.at[0], own_sem.at[2])]
    back_into(2, h_ref, s_ref, q_ref, zt, ey, send2[1], 0, rim_ref, first)
    send2[1][:, 3, :] = rim_ref[...]
    owns.append(exchange(send2[1], recv2[1], ss_2.at[1], rs_2.at[1], own_sem.at[3]))
    for k in range(2):
        finish(owns[k], send2[k], recv2[k], ss_2.at[k], rs_2.at[k])
    lane = lanes(SLOTS)
    rims = recv2[1][:, 3, :]
    for a in range(3):
        from_ref, at = recv2[a // 2], 3 * (a % 2)
        shared = from_ref[:, at + 2, :]
        parts = []
        for part in range(2):
            rest = jnp.where(lane < 80, turn(rims, 64 - 16 * (2 * a + part)), 0.0)
            rest = jnp.where(lane < 64, turn(shared, -64 * part), rest)
            parts.append(jnp.concatenate([from_ref[:, at + part, :], rest], axis=1))
        field = dot3((xi[0][...], xi[1][...]), split(jnp.concatenate(parts, axis=0)))
        top = jnp.max(jnp.max(jnp.abs(field), axis=0, keepdims=True), axis=1, keepdims=True)
        top = jnp.maximum(top, 1e-30)
        field = field / top
        hi = field.astype(BF).astype(F32)
        here = slice(128 * a, 128 * a + 128)
        ft_ref[here] = (hi * 65536.0).astype(BF)
        f8_ref[here, :PAD] = ((field - hi) * 65536.0).astype(F8)
        f8_ref[here, PAD:] = (hi * 16.0).astype(F8)
        scale_ref[a : a + 1] = jnp.broadcast_to(top * (1.0 / 65536.0), (1, 128))
        for i, (v, o) in enumerate(((ft_ref, ft_out), (f8_ref, f8_out))):
            leaving.append(pltpu.make_async_copy(v.at[here], o.at[here], out_sem.at[1 + 2 * a + i]))
            leaving[-1].start()
    scale_ref[3:] = jnp.zeros((5, 128), F32)
    leaving.append(pltpu.make_async_copy(scale_ref, scale_out, out_sem.at[7]))
    leaving[-1].start()
    for copy in leaving:
        copy.wait()


def field_of(operands, blk=4096, n=512):
    ops = [o.reshape(1, -1) if o.ndim == 1 else o for o in operands]
    assert len(ops) == N_IN
    cap = 128
    dma = pltpu.SemaphoreType.DMA
    return pl.pallas_call(
        functools.partial(field_kernel, n=n),
        name="field",
        out_shape=(
            jax.ShapeDtypeStruct((384, PAD), BF),
            jax.ShapeDtypeStruct((384, 2 * PAD), F8),
            jax.ShapeDtypeStruct((8, 128), F32),
            jax.ShapeDtypeStruct((9, N_COL * cap), F32),
        ),
        in_specs=[pl.BlockSpec(memory_space=pltpu.MemorySpace.HBM)] * N_IN,
        out_specs=(pl.BlockSpec(memory_space=pltpu.MemorySpace.HBM),) * 4,
        scratch_shapes=[pltpu.VMEM(o.shape, o.dtype) for o in ops]
        + [
            pltpu.VMEM((3 * 512, ops[0].shape[1]), BF),
            pltpu.VMEM((N_COL, 9, cap), F32),
            pltpu.VMEM((N_COL, 9, cap), F32),
            pltpu.VMEM((2 * ROWS, blk), BF),
            pltpu.VMEM((256, blk), BF),
            pltpu.VMEM((2 * ROWS, 256), F32),
            pltpu.VMEM((SLOTS, 4, 128), F32),
            pltpu.VMEM((SLOTS, 4, 128), F32),
            pltpu.VMEM((3, 4, 256, 256), F32),
            pltpu.VMEM((2, 384, PAD), BF),
            pltpu.VMEM((4, 256, 256), F32),
            pltpu.VMEM((2, 256, 256), F32),
            pltpu.VMEM((SLOTS, 6, 128), F32),
            pltpu.VMEM((SLOTS, 4, 128), F32),
            pltpu.VMEM((SLOTS, 6, 128), F32),
            pltpu.VMEM((SLOTS, 4, 128), F32),
            pltpu.VMEM((SLOTS, 128), F32),
            pltpu.VMEM((384, PAD), BF),
            pltpu.VMEM((384, 2 * PAD), F8),
            pltpu.VMEM((8, 128), F32),
            pltpu.VMEM((9, N_COL * cap), F32),
            pltpu.SemaphoreType.REGULAR,
            dma((N_IN,)),
            dma((5,)),
            dma(()),
            dma(()),
            dma(()),
            dma(()),
            dma((2,)),
            dma((2,)),
            dma((8,)),
        ],
        compiler_params=pltpu.CompilerParams(vmem_limit_bytes=BIG, has_side_effects=True, collective_id=0),
    )(*ops)


def body(
    resident_cell,
    resident_corner,
    resident_frac,
    resident_charge,
    resident_momentum,
    migrant_dest,
    migrant_cell,
    migrant_corner,
    migrant_frac,
    migrant_charge,
    migrant_momentum,
    green,
):
    consts = [jnp.asarray(t) for pair in tables() for t in pair]
    stayed = (resident_cell, resident_corner, resident_frac, resident_charge)
    *field, moved = field_of(
        [
            migrant_dest.reshape(-1),
            migrant_cell,
            migrant_corner,
            migrant_frac,
            migrant_charge,
            migrant_momentum,
            *stayed,
            green,
            *consts,
        ]
    )
    return kick(field, moved, *stayed, resident_momentum)


def solution(mesh):
    both = ("row", "col")
    in_specs = (
        P(both),
        P(both),
        P(None, both),
        P(both),
        P(None, both),
        P(both, None),
        P(both),
        P(both),
        P(None, both),
        P(both),
        P(None, both),
        P(None, None, both, None, None),
    )
    out_specs = (P(None, both), P(None, both))
    return jax.shard_map(body, mesh=mesh, in_specs=in_specs, out_specs=out_specs, check_vma=False)
```

```python
import functools

import jax
import jax.numpy as jnp
import numpy as np
from jax import lax
from jax.experimental import pallas as pl
from jax.experimental.pallas import tpu as pltpu
from jax.sharding import PartitionSpec as P

F32, BF, I32, F8 = jnp.float32, jnp.bfloat16, jnp.int32, jnp.float8_e4m3fn
N_ROW, N_COL = 4, 32
SLOTS = N_ROW * N_COL
ROWS = 208
PAD = 256
BIG = 60 << 20


def split_np(table):
    hi = table.astype(jnp.bfloat16)
    return hi, (table - hi.astype(np.float64)).astype(jnp.bfloat16)


def y_places():
    y = np.full(PAD, -1)
    y[:128] = np.arange(128)
    for r in range(N_ROW):
        for side in range(2):
            first = 128 + 16 * r + 8 * side
            y[first : first + 6] = 32 * r + 33 * side - 1
    return y


def tables():
    wave = np.arange(256)
    y = y_places()[:, None]
    angle = 2 * np.pi / 256 * (y * wave % 256)
    live = (y >= 0) & (y < 128)
    ey = np.concatenate([np.cos(angle), np.sin(angle)], axis=1) * live
    zg = (4 * np.arange(N_COL)[None] + np.arange(6)[:, None] - 1).reshape(-1)
    live = ((zg >= 0) & (zg < 128))[None]
    angle = 2 * np.pi / 256 * (wave[:, None] * zg % 256)
    ez = np.stack([np.cos(angle) * live, np.sin(angle) * live])
    ezt = ez.transpose(0, 2, 1).reshape(384, 256)
    x, j = np.arange(128), np.arange(128)
    angle = 2 * np.pi / 256 * (j[:, None] * x % 256)
    imag = -np.sin(angle)
    imag[0] = 1 - 2 * (x % 2)
    dx = np.concatenate([np.cos(angle), imag])
    return [split_np(t) for t in (ey, ez.reshape(512, 192), ezt, dx, dx.T / 256.0**3)]


def split(v):
    hi = v.astype(BF)
    return hi, (v - hi.astype(F32)).astype(BF)


def dot3(a, b, dims=((1,), (0,))):
    one = lambda p, q: lax.dot_general(p, q, (dims, ((), ())), preferred_element_type=F32)
    return one(a[0], b[0]) + (one(a[0], b[1]) + one(a[1], b[0]))


def tile16(row, n):
    return jnp.broadcast_to(row, (16, n)).astype(BF)


def yz_weights(cell, corner, fy, fz, q, n, write):
    y = (cell >> 7) & 31
    z = (cell >> 12) + 1
    yfar = y + ((corner >> 1) & 1) * 2 - 1
    zfar = z + ((corner >> 2) & 1) * 2 - 1
    io8 = lax.broadcasted_iota(I32, (8, n), 0)
    wz = jnp.where(io8 == z, (1.0 - fz) * q, jnp.where(io8 == zfar, fz * q, 0.0))
    near = wz * (1.0 - fy)
    far = wz * fy
    nh = near.astype(BF).astype(F32); nl = near - nh
    fh = far.astype(BF).astype(F32); fl = far - fh
    io16 = lax.broadcasted_iota(I32, (16, n), 0).astype(BF)
    yb = jnp.broadcast_to(y.astype(F32), (16, n)).astype(BF)
    yfb = jnp.broadcast_to(yfar.astype(F32), (16, n)).astype(BF)
    zero = jnp.zeros((16, n), BF)
    masks = [(yb == io16, yfb == io16), (yb == io16 + 16.0, yfb == io16 + 16.0)]
    for ze in range(6):
        a, b, c, d = (tile16(v[ze:ze+1], n) for v in (nh, fh, nl, fl))
        for h in range(2):
            mn, mf = masks[h]
            write(ze*32 + h*16, jnp.where(mn, a, jnp.where(mf, b, zero)), jnp.where(mn, c, jnp.where(mf, d, zero)))
    isb = yfar < 0
    isa = yfar > 31
    rh = jnp.concatenate([jnp.where(isb, fh, 0.0), jnp.where(isa, fh, 0.0)], axis=0).astype(BF)
    rl = jnp.concatenate([jnp.where(isb, fl, 0.0), jnp.where(isa, fl, 0.0)], axis=0).astype(BF)
    write(192, rh, rl)

def x_weights(cell, corner, fx, n, write):
    x = cell & 127
    xfar = x + (corner & 1) * 2 - 1
    gx = 1.0 - fx
    gh = gx.astype(BF).astype(F32)
    fh = fx.astype(BF).astype(F32)
    gh, gl, fh, fl = (tile16(v, n) for v in (gh, gx - gh, fh, fx - fh))
    io16 = lax.broadcasted_iota(I32, (16, n), 0).astype(BF)
    xb, xfb = tile16(x.astype(F32), n), tile16(xfar.astype(F32), n)
    zero = jnp.zeros((16, n), BF)
    for t in range(8):
        near, far = xb == io16 + BF(16 * t), xfb == io16 + BF(16 * t)
        write(16 * t, jnp.where(near, gh, jnp.where(far, fh, zero)), jnp.where(near, gl, jnp.where(far, fl, zero)))


def deposit_block(rows, a_ref, b_ref, acc_ref, n):
    for s in range(a_ref.shape[1] // n):
        here = pl.ds(s * n, n)
        cell, corner, fx, fy, fz, q = rows(s)

        def write_a(r, hi, lo):
            a_ref[r : r + 16, here] = hi
            a_ref[ROWS + r : ROWS + r + 16, here] = lo

        def write_b(r, hi, lo):
            b_ref[r : r + 16, here] = hi
            b_ref[128 + r : 128 + r + 16, here] = lo

        yz_weights(cell, corner, fy, fz, q, n, write_a)
        x_weights(cell, corner, fx, n, write_b)
    acc_ref[...] += lax.dot_general(a_ref[...], b_ref[...], (((1,), (1,)), ((), ())), preferred_element_type=F32)


def pack_into(dest_ref, cell_ref, corner_ref, frac_ref, q_ref, mom_ref, lhs_ref, out_ref):
    total = dest_ref.shape[-1]
    dest = dest_ref[...]
    hits = (lax.broadcasted_iota(I32, (N_COL, total), 0) == dest).astype(F32)
    upper = (lax.broadcasted_iota(I32, (256, 256), 0) < lax.broadcasted_iota(I32, (256, 256), 1)).astype(BF)
    carry = jnp.zeros((N_COL, 1), F32)
    ranks = []
    for s in range(0, total, 256):
        part = hits[:, s : s + 256]
        before = jnp.dot(part.astype(BF), upper, preferred_element_type=F32) + carry
        carry = carry + jnp.sum(part, axis=1, keepdims=True)
        ranks.append(jnp.sum(part * before, axis=0, keepdims=True))
    rank = jnp.concatenate(ranks, axis=1)
    cap = out_ref.shape[-1]
    choose = (lax.broadcasted_iota(I32, (cap, total), 0).astype(F32) == rank).astype(BF)
    payload = jnp.concatenate(
        [
            frac_ref[...],
            q_ref[...],
            mom_ref[...],
            cell_ref[...].astype(F32),
            corner_ref[...].astype(F32),
            jnp.zeros((7, total), F32),
        ],
        axis=0,
    )
    hi = payload.astype(BF)
    rest = payload - hi.astype(F32)
    mid = rest.astype(BF)
    low = (rest - mid.astype(F32)).astype(BF)
    destb = tile16(dest.astype(F32), total)
    zero = jnp.zeros((16, total), BF)
    for d in range(N_COL):
        mask = destb == BF(d)
        for i, piece in enumerate((hi, mid, low)):
            lhs_ref[i * 512 + d * 16 : i * 512 + d * 16 + 16] = jnp.where(mask, piece, zero)
    got = lax.dot_general(lhs_ref[...], choose, (((1,), (1,)), ((), ())), preferred_element_type=F32)
    got = (got[:512] + got[512:1024]) + got[1024:]
    for d in range(N_COL):
        out_ref[d] = got[d * 16 : d * 16 + 9]


def yz_tiles(cell, corner, fy, fz, q, n, write):
    y = (cell >> 7) & 31
    z = (cell >> 12) + 1
    yfar = y + ((corner >> 1) & 1) * 2 - 1
    zfar = z + ((corner >> 2) & 1) * 2 - 1
    io8 = lax.broadcasted_iota(I32, (8, n), 0)
    wz = jnp.where(io8 == z, (1.0 - fz) * q, jnp.where(io8 == zfar, fz * q, 0.0))
    near = wz * (1.0 - fy)
    far = wz * fy
    nh = near.astype(BF).astype(F32)
    fh = far.astype(BF).astype(F32)
    nl, fl = (near - nh) * 4096.0, (far - fh) * 4096.0

    def big(row):
        half = tile16(row, n)
        return jnp.concatenate([half, half], axis=0)

    io = lax.broadcasted_iota(I32, (32, n), 0).astype(F32).astype(BF)
    at_near, at_far = big(y.astype(F32)) == io, big(yfar.astype(F32)) == io
    zero = jnp.zeros((32, n), BF)
    for ze in range(6):
        a, b, c, d = (big(v[ze : ze + 1]) for v in (nh, fh, nl, fl))
        write(ze * 32, jnp.where(at_near, a, jnp.where(at_far, b, zero)), jnp.where(at_near, c, jnp.where(at_far, d, zero)))
    below, above = yfar < 0, yfar > 31
    rims = [
        jnp.concatenate([jnp.where(below, v, 0.0), jnp.where(above, v, 0.0), jnp.zeros((16, n), F32)], axis=0)
        for v in (fh, fl)
    ]
    write(192, rims[0].astype(BF), rims[1].astype(BF))


def kick_chunk(ft_ref, f8_ref, w_ref, w8_ref, here, n, rows):
    cell, corner, fx, fy, fz, q = rows

    def write(r, hi, lo):
        w_ref[r : r + 32, here] = hi
        w8_ref[r : r + 32, here] = hi.astype(F8)
        w8_ref[PAD + r : PAD + r + 32, here] = lo.astype(F8)

    yz_tiles(cell, corner, fy, fz, q, n, write)
    got = jnp.dot(ft_ref[...], w_ref[:, here], preferred_element_type=F32)
    more = jnp.dot(f8_ref[...], w8_ref[:, here], preferred_element_type=F32)
    x = cell & 127
    xfar = x + (corner & 1) * 2 - 1
    io = lax.broadcasted_iota(I32, (128, n), 0)
    wx = jnp.where(io == x, 1.0 - fx, jnp.where(io == xfar, fx, 0.0))
    total = got + more
    return [jnp.sum(total[a * 128 : a * 128 + 128] * wx, axis=0, keepdims=True) for a in range(3)]


def kick_kernel(*refs, n):
    hbm, (out_hbm, migrant_hbm), held = refs[:9], refs[9:11], refs[11:20]
    out_ref, migrant_ref, w_ref, w8_ref, made_sem, in_sem, out_sem, migrant_sem = refs[20:]
    made = [pltpu.make_async_copy(hbm[i], held[i], made_sem.at[i]) for i in range(4)]
    for copy in made:
        copy.start()
    (ft_ref, f8_ref, scale_ref, moved_ref), hbm, held = held[:4], hbm[4:], held[4:]
    cell_ref, corner_ref, frac_ref, q_ref, mom_ref = held
    blk = w_ref.shape[1]
    total = cell_ref.shape[1]
    pieces = (pl.ds(0, blk), pl.ds(blk, total - blk))
    copies = [
        [pltpu.make_async_copy(h.at[:, p], v.at[:, p], in_sem.at[j, i]) for i, (h, v) in enumerate(zip(hbm, held))]
        for j, p in enumerate(pieces)
    ]
    for copy in copies[0] + copies[1]:
        copy.start()
    for r in (224, 480):
        w8_ref[r : r + 32] = jnp.zeros((32, blk), F8)
    w_ref[224:] = jnp.zeros((32, blk), BF)
    chunk = functools.partial(kick_chunk, ft_ref, f8_ref, w_ref, w8_ref)
    for copy in made:
        copy.wait()

    for s in range(moved_ref.shape[1] // n):
        here = pl.ds(s * n, n)
        got = moved_ref[:, here]
        rows = (got[7:8].astype(I32), got[8:9].astype(I32), got[0:1], got[1:2], got[2:3], got[3:4])
        kicks = chunk(here, n, rows)
        for a in range(3):
            migrant_ref[a : a + 1, here] = got[4 + a : 5 + a] + kicks[a] * scale_ref[a : a + 1, 0:1]
    migrant_out = pltpu.make_async_copy(migrant_ref, migrant_hbm, migrant_sem)
    migrant_out.start()
    for copy in copies[0]:
        copy.wait()

    def residents(i, _):
        @pl.when(i == 1)
        def _():
            for copy in copies[1]:
                copy.wait()

        for s in range(blk // n):
            here = pl.ds(pl.multiple_of(i * blk + s * n, n), n)
            rows = (
                cell_ref[:, here],
                corner_ref[:, here],
                frac_ref[0:1, here],
                frac_ref[1:2, here],
                frac_ref[2:3, here],
                q_ref[:, here],
            )
            kicks = chunk(pl.ds(s * n, n), n, rows)
            for a in range(3):
                out_ref[a : a + 1, here] = mom_ref[a : a + 1, here] + kicks[a] * scale_ref[a : a + 1, 0:1]
        block = pl.ds(pl.multiple_of(i * blk, blk), blk)
        pltpu.make_async_copy(out_ref.at[:, block], out_hbm.at[:, block], out_sem).start()
        return 0

    lax.fori_loop(0, total // blk, residents, 0)
    migrant_out.wait()
    pltpu.make_async_copy(out_ref, out_hbm, out_sem).wait()


def kick(tables_of, moved, cell, corner, frac, q, mom, blk=8192, n=256):
    ops = [*tables_of, moved, cell.reshape(1, -1), corner.reshape(1, -1), frac, q.reshape(1, -1), mom]
    hbm = pl.BlockSpec(memory_space=pltpu.MemorySpace.HBM)
    return pl.pallas_call(
        functools.partial(kick_kernel, n=n),
        name="kick",
        out_shape=(jax.ShapeDtypeStruct(mom.shape, F32), jax.ShapeDtypeStruct((3, moved.shape[1]), F32)),
        in_specs=[hbm] * 9,
        out_specs=(hbm, hbm),
        scratch_shapes=[pltpu.VMEM(o.shape, o.dtype) for o in ops]
        + [
            pltpu.VMEM(mom.shape, F32),
            pltpu.VMEM((3, moved.shape[1]), F32),
            pltpu.VMEM((PAD, blk), BF),
            pltpu.VMEM((2 * PAD, blk), F8),
            pltpu.SemaphoreType.DMA((4,)),
            pltpu.SemaphoreType.DMA((2, 5)),
            pltpu.SemaphoreType.DMA(()),
            pltpu.SemaphoreType.DMA(()),
        ],
        compiler_params=pltpu.CompilerParams(vmem_limit_bytes=BIG),
    )(*ops)


def green_into(green_ref, h_ref, first):
    index = lax.broadcasted_iota(I32, (256, 256), 0) + lax.broadcasted_iota(I32, (256, 256), 1)
    mirror = ((index == 0) | (index == 256)).astype(BF)

    def flip(plane):
        half = jnp.dot(mirror, plane, preferred_element_type=F32).astype(BF)
        return jnp.dot(half, mirror, preferred_element_type=F32)

    @pl.when(first)
    def _():
        for a in range(3):
            for sign in range(2):
                real, imag = green_ref[a, 0, sign], green_ref[a, 1, sign]
                h_ref[a, 2 * sign] = 0.5 * (real.astype(F32) + flip(real))
                h_ref[a, 2 * sign + 1] = 0.5 * (imag.astype(F32) - flip(imag))

    @pl.when(jnp.logical_not(first))
    def _():
        for a in range(3):
            h_ref[a, 0] = green_ref[a, 0, 0].astype(F32) + flip(green_ref[a, 0, 1])
            h_ref[a, 1] = green_ref[a, 1, 0].astype(F32) - flip(green_ref[a, 1, 1])


def lanes(rows):
    return lax.broadcasted_iota(I32, (rows, 128), 1)


def turn(v, by):
    by = by % 128
    return pltpu.roll(v, by, 1) if by else v


def forward_into(got_ref, ey, ez, lhs_ref, s_ref, first):
    lane = lanes(N_COL)
    for part in range(2):
        inner = [jnp.zeros((N_COL, 128), F32)] * 6
        rims = jnp.zeros((N_COL, 128), F32)
        for r in range(N_ROW):
            rows = slice(32 * r, 32 * r + 32)
            low, high = got_ref[rows, 2 * part, :], got_ref[rows, 2 * part + 1, :]
            for ze in range(6):
                moved = turn(low if ze < 4 else high, 32 * (r - ze % 4))
                inner[ze] = jnp.where(lane // 32 == r, moved, inner[ze])
            rims = jnp.where(lane // 16 == r, turn(high, 16 * r - 64), rims)
        for ze in range(6):
            where = slice(192 * part + 32 * ze, 192 * part + 32 * ze + 32)
            for k, v in enumerate((inner[ze], jnp.where(lane % 8 == ze, rims, 0.0))):
                hi, lo = split(v)
                lhs_ref[0, where, 128 * k : 128 * k + 128] = hi
                lhs_ref[1, where, 128 * k : 128 * k + 128] = lo
    u = dot3((lhs_ref[0], lhs_ref[1]), (ey[0][...], ey[1][...]))
    re_c, re_s, im_c, im_s = u[:192, :256], u[:192, 256:], u[192:, :256], u[192:, 256:]
    ezs = (ez[0][...], ez[1][...])

    def forward(real, imag):
        v = dot3(ezs, split(jnp.concatenate([real, imag], axis=1)))
        return v[:256, :256] + v[256:, 256:], v[:256, 256:] - v[256:, :256]

    @pl.when(first)
    def _():
        s_ref[0], s_ref[1] = forward(re_c, -re_s)
        s_ref[2], s_ref[3] = forward(im_c, -im_s)

    @pl.when(jnp.logical_not(first))
    def _():
        s_ref[0], s_ref[1] = forward(re_c + im_s, im_c - re_s)


def back_into(a, h_ref, s_ref, q_ref, zt, ey, out_ref, at, rim_ref, first):
    a_re = s_ref[0] * h_ref[a, 0] - s_ref[1] * h_ref[a, 1]
    a_im = s_ref[0] * h_ref[a, 1] + s_ref[1] * h_ref[a, 0]
    q_ref[0], q_ref[1] = a_re, a_im

    @pl.when(first)
    def _():
        b_re = s_ref[2] * h_ref[a, 2] - s_ref[3] * h_ref[a, 3]
        b_im = s_ref[2] * h_ref[a, 3] + s_ref[3] * h_ref[a, 2]
        q_ref[0] = q_ref[0] - b_im
        q_ref[1] = q_ref[1] + b_re

    q = split(jnp.concatenate([q_ref[0], q_ref[1]], axis=1))
    v = dot3((zt[0][...], zt[1][...]), q)
    v = split(jnp.concatenate([v[:192, :256] - v[192:, 256:], v[:192, 256:] + v[192:, :256]], axis=0))
    cos = dot3(v, (ey[0][:, :256], ey[1][:, :256]), ((1,), (1,)))
    sin = dot3(v, (ey[0][:, 256:], ey[1][:, 256:]), ((1,), (1,)))
    w = (cos[:192] - sin[192:], cos[192:] + sin[:192])
    lane = lanes(N_COL)
    rims = []
    for part in range(2):
        rim = jnp.zeros((N_COL, 128), F32)
        for ze in range(6):
            rim = jnp.where(lane % 8 == ze, w[part][32 * ze : 32 * ze + 32, 128:], rim)
        rims.append(rim)
    for r in range(N_ROW):
        rows = slice(32 * r, 32 * r + 32)
        shared = jnp.zeros((N_COL, 128), F32)
        for part in range(2):
            mine = jnp.zeros((N_COL, 128), F32)
            for ze in range(6):
                to = ze if ze < 4 else ze - 4 + 2 * part
                moved = turn(w[part][32 * ze : 32 * ze + 32, :128], 32 * (to - r))
                if ze < 4:
                    mine = jnp.where(lane // 32 == to, moved, mine)
                else:
                    shared = jnp.where(lane // 32 == to, moved, shared)
            out_ref[rows, at + part, :] = mine
            to = 2 * a + part
            old = rim_ref[rows]
            rim_ref[rows] = jnp.where(lane // 16 == to, turn(rims[part], 16 * (to - r)), old)
        out_ref[rows, at + 2, :] = shared


MESH = pl.DeviceIdType.MESH
N_IN = 21


def field_kernel(*refs, n):
    hbm, (ft_out, f8_out, scale_out, moved_out) = refs[:N_IN], refs[N_IN : N_IN + 4]
    held = refs[N_IN + 4 : 2 * N_IN + 4]
    (lhs_p, pack_s, pack_r, a_ref, b_ref, acc_ref, send1, recv1, h_ref, lhs_f, s_ref, q_ref, *late) = refs[
        2 * N_IN + 4 : 2 * N_IN + 25
    ]
    send2, recv2, rim_ref = late[:2], late[2:4], late[4]
    ft_ref, f8_ref, scale_ref, moved_ref = late[5:]
    meet, in_sem, own_sem, ss_m, rs_m, ss_1, rs_1, ss_2, rs_2, out_sem = refs[2 * N_IN + 25 :]
    row, col = lax.axis_index("row"), lax.axis_index("col")
    me = row * N_COL + col
    first = me == 0

    def device(d):
        return (d >> 5, d & 31)

    copies = [pltpu.make_async_copy(h, v, in_sem.at[i]) for i, (h, v) in enumerate(zip(hbm, held))]
    for copy in copies[:6]:
        copy.start()

    barrier = pltpu.get_barrier_semaphore()

    def greet_row(sem):
        for i in range(1, N_ROW):
            pl.semaphore_signal(sem, inc=1, device_id=((row + i) & 3, col), device_id_type=MESH)

    def greet_col(i, _):
        pl.semaphore_signal(barrier, inc=1, device_id=(row, (col + i) & 31), device_id_type=MESH)
        return 0

    greet_row(barrier)
    lax.fori_loop(1, N_COL, greet_col, 0, unroll=8)
    for copy in copies[6:]:
        copy.start()
    acc_ref[...] = jnp.zeros_like(acc_ref)

    for copy in copies[:6]:
        copy.wait()
    pack_into(*held[:6], lhs_p, pack_s)
    for copy in copies[6:10]:
        copy.wait()
    cell_ref, corner_ref, frac_ref, q_in = held[6:10]
    blk = a_ref.shape[2]
    steps = cell_ref.shape[1] // (2 * blk)

    def resident(i, _):
        for k in range(2):

            def rows(s, k=k):
                here = pl.ds(pl.multiple_of((2 * i + k) * blk + s * n, n), n)
                return (
                    cell_ref[:, here],
                    corner_ref[:, here],
                    frac_ref[0:1, here],
                    frac_ref[1:2, here],
                    frac_ref[2:3, here],
                    q_in[:, here],
                )

            deposit_block(rows, a_ref.at[k], b_ref.at[k], acc_ref, n)
        return 0

    lax.fori_loop(0, steps // 2, resident, 0)
    pl.semaphore_wait(barrier, N_ROW - 1 + N_COL - 1)
    greet_row(meet)

    def send_migrants(i, _):
        c = (col + i) & 31
        pltpu.make_async_remote_copy(
            src_ref=pack_s.at[c],
            dst_ref=pack_r.at[col],
            send_sem=ss_m,
            recv_sem=rs_m,
            device_id=(row, c),
            device_id_type=MESH,
        ).start()
        return 0

    lax.fori_loop(1, N_COL, send_migrants, 0, unroll=8)
    own = pltpu.make_async_copy(pack_s.at[col], pack_r.at[col], own_sem.at[0])
    own.start()
    lax.fori_loop(steps // 2, steps, resident, 0)
    own.wait()
    rest = pl.ds(0, N_COL - 1)
    pltpu.make_async_remote_copy(
        src_ref=pack_s.at[rest],
        dst_ref=pack_r.at[rest],
        send_sem=ss_m,
        recv_sem=rs_m,
        device_id=(row, col),
        device_id_type=MESH,
    ).wait()
    for s in range(N_COL):
        moved_ref[:, 128 * s : 128 * s + 128] = pack_r[s]
    leaving = [pltpu.make_async_copy(moved_ref, moved_out, out_sem.at[0])]
    leaving[0].start()

    def migrant(i, _):
        def rows(s):
            here = pl.ds(pl.multiple_of(i * blk + s * n, n), n)
            got = moved_ref[:, here]
            return (
                got[7:8].astype(I32),
                got[8:9].astype(I32),
                got[0:1],
                got[1:2],
                got[2:3],
                got[3:4],
            )

        deposit_block(rows, a_ref.at[0], b_ref.at[0], acc_ref, n)
        return 0

    lax.fori_loop(0, moved_ref.shape[1] // blk, migrant, 0)
    for copy in copies[10:]:
        copy.wait()
    green_ref = held[10]
    ey, ez, zt, dx, xi = (held[11 + 2 * i : 13 + 2 * i] for i in range(5))

    acc = acc_ref[...]
    grid = (acc[:ROWS, :128] + acc[ROWS:, 128:]) + (acc[:ROWS, 128:] + acc[ROWS:, :128])
    sent = dot3((dx[0][...], dx[1][...]), split(grid), ((1,), (1,)))
    sent = jnp.concatenate([sent, jnp.zeros((256, PAD - ROWS), F32)], axis=1)
    for part in range(2):
        for half in range(2):
            send1[:, 2 * part + half, :] = sent[128 * part : 128 * part + 128, 128 * half : 128 * half + 128]

    def exchange(src, dst, ss, rs, own_at):
        def go(i, _):
            d = (me + i) & 127
            pltpu.make_async_remote_copy(
                src_ref=src.at[d],
                dst_ref=dst.at[me],
                send_sem=ss,
                recv_sem=rs,
                device_id=device(d),
                device_id_type=MESH,
            ).start()
            return 0

        lax.fori_loop(1, SLOTS, go, 0, unroll=8)
        own = pltpu.make_async_copy(src.at[me], dst.at[me], own_at)
        own.start()
        return own

    def finish(own, src, dst, ss, rs):
        own.wait()
        rest = pl.ds(0, SLOTS - 1)
        pltpu.make_async_remote_copy(
            src_ref=src.at[rest],
            dst_ref=dst.at[rest],
            send_sem=ss,
            recv_sem=rs,
            device_id=(row, col),
            device_id_type=MESH,
        ).wait()

    pl.semaphore_wait(meet, N_ROW - 1)
    own = exchange(send1, recv1, ss_1, rs_1, own_sem.at[1])
    green_into(green_ref, h_ref, first)
    finish(own, send1, recv1, ss_1, rs_1)
    forward_into(recv1, ey, ez, lhs_f, s_ref, first)
    rim_ref[...] = jnp.zeros_like(rim_ref)
    back_into(0, h_ref, s_ref, q_ref, zt, ey, send2[0], 0, rim_ref, first)
    back_into(1, h_ref, s_ref, q_ref, zt, ey, send2[0], 3, rim_ref, first)
    owns = [exchange(send2[0], recv2[0], ss_2.at[0], rs_2.at[0], own_sem.at[2])]
    back_into(2, h_ref, s_ref, q_ref, zt, ey, send2[1], 0, rim_ref, first)
    send2[1][:, 3, :] = rim_ref[...]
    owns.append(exchange(send2[1], recv2[1], ss_2.at[1], rs_2.at[1], own_sem.at[3]))
    for k in range(2):
        finish(owns[k], send2[k], recv2[k], ss_2.at[k], rs_2.at[k])
    lane = lanes(SLOTS)
    rims = recv2[1][:, 3, :]
    for a in range(3):
        from_ref, at = recv2[a // 2], 3 * (a % 2)
        shared = from_ref[:, at + 2, :]
        parts = []
        for part in range(2):
            rest = jnp.where(lane < 80, turn(rims, 64 - 16 * (2 * a + part)), 0.0)
            rest = jnp.where(lane < 64, turn(shared, -64 * part), rest)
            parts.append(jnp.concatenate([from_ref[:, at + part, :], rest], axis=1))
        field = dot3((xi[0][...], xi[1][...]), split(jnp.concatenate(parts, axis=0)))
        top = jnp.max(jnp.max(jnp.abs(field), axis=0, keepdims=True), axis=1, keepdims=True)
        top = jnp.maximum(top, 1e-30)
        field = field / top
        hi = field.astype(BF).astype(F32)
        here = slice(128 * a, 128 * a + 128)
        ft_ref[here] = (hi * 65536.0).astype(BF)
        f8_ref[here, :PAD] = ((field - hi) * 65536.0).astype(F8)
        f8_ref[here, PAD:] = (hi * 16.0).astype(F8)
        scale_ref[a : a + 1] = jnp.broadcast_to(top * (1.0 / 65536.0), (1, 128))
        for i, (v, o) in enumerate(((ft_ref, ft_out), (f8_ref, f8_out))):
            leaving.append(pltpu.make_async_copy(v.at[here], o.at[here], out_sem.at[1 + 2 * a + i]))
            leaving[-1].start()
    scale_ref[3:] = jnp.zeros((5, 128), F32)
    leaving.append(pltpu.make_async_copy(scale_ref, scale_out, out_sem.at[7]))
    leaving[-1].start()
    for copy in leaving:
        copy.wait()


def field_of(operands, blk=4096, n=512):
    ops = [o.reshape(1, -1) if o.ndim == 1 else o for o in operands]
    assert len(ops) == N_IN
    cap = 128
    dma = pltpu.SemaphoreType.DMA
    return pl.pallas_call(
        functools.partial(field_kernel, n=n),
        name="field",
        out_shape=(
            jax.ShapeDtypeStruct((384, PAD), BF),
            jax.ShapeDtypeStruct((384, 2 * PAD), F8),
            jax.ShapeDtypeStruct((8, 128), F32),
            jax.ShapeDtypeStruct((9, N_COL * cap), F32),
        ),
        in_specs=[pl.BlockSpec(memory_space=pltpu.MemorySpace.HBM)] * N_IN,
        out_specs=(pl.BlockSpec(memory_space=pltpu.MemorySpace.HBM),) * 4,
        scratch_shapes=[pltpu.VMEM(o.shape, o.dtype) for o in ops]
        + [
            pltpu.VMEM((3 * 512, ops[0].shape[1]), BF),
            pltpu.VMEM((N_COL, 9, cap), F32),
            pltpu.VMEM((N_COL, 9, cap), F32),
            pltpu.VMEM((2, 2 * ROWS, blk), BF),
            pltpu.VMEM((2, 256, blk), BF),
            pltpu.VMEM((2 * ROWS, 256), F32),
            pltpu.VMEM((SLOTS, 4, 128), F32),
            pltpu.VMEM((SLOTS, 4, 128), F32),
            pltpu.VMEM((3, 4, 256, 256), F32),
            pltpu.VMEM((2, 384, PAD), BF),
            pltpu.VMEM((4, 256, 256), F32),
            pltpu.VMEM((2, 256, 256), F32),
            pltpu.VMEM((SLOTS, 6, 128), F32),
            pltpu.VMEM((SLOTS, 4, 128), F32),
            pltpu.VMEM((SLOTS, 6, 128), F32),
            pltpu.VMEM((SLOTS, 4, 128), F32),
            pltpu.VMEM((SLOTS, 128), F32),
            pltpu.VMEM((384, PAD), BF),
            pltpu.VMEM((384, 2 * PAD), F8),
            pltpu.VMEM((8, 128), F32),
            pltpu.VMEM((9, N_COL * cap), F32),
            pltpu.SemaphoreType.REGULAR,
            dma((N_IN,)),
            dma((5,)),
            dma(()),
            dma(()),
            dma(()),
            dma(()),
            dma((2,)),
            dma((2,)),
            dma((8,)),
        ],
        compiler_params=pltpu.CompilerParams(vmem_limit_bytes=BIG, has_side_effects=True, collective_id=0),
    )(*ops)


def body(
    resident_cell,
    resident_corner,
    resident_frac,
    resident_charge,
    resident_momentum,
    migrant_dest,
    migrant_cell,
    migrant_corner,
    migrant_frac,
    migrant_charge,
    migrant_momentum,
    green,
):
    consts = [jnp.asarray(t) for pair in tables() for t in pair]
    stayed = (resident_cell, resident_corner, resident_frac, resident_charge)
    *field, moved = field_of(
        [
            migrant_dest.reshape(-1),
            migrant_cell,
            migrant_corner,
            migrant_frac,
            migrant_charge,
            migrant_momentum,
            *stayed,
            green,
            *consts,
        ]
    )
    return kick(field, moved, *stayed, resident_momentum)


def solution(mesh):
    both = ("row", "col")
    in_specs = (
        P(both),
        P(both),
        P(None, both),
        P(both),
        P(None, both),
        P(both, None),
        P(both),
        P(both),
        P(None, both),
        P(both),
        P(None, both),
        P(None, None, both, None, None),
    )
    out_specs = (P(None, both), P(None, both))
    return jax.shard_map(body, mesh=mesh, in_specs=in_specs, out_specs=out_specs, check_vma=False)
```
